32 devices in a mesh: groups: 2 (over x), seq: 16 (over z, y, core).
Axes of the slice: x: 2, y: 2, z: 4, core: 2. Of those that a mesh axis runs over, the one named last changes fastest.
Arguments:
- prefill_q: bfloat16 [128, 4096], P(('groups', 'seq')), parts along dimension 0, may hold values from -128 to 128
- prefill_k: bfloat16 [8192, 1024], P(('groups', 'seq')), parts along dimension 0, may hold values from -6 to 6
- prefill_v: bfloat16 [8192, 1024], P(('groups', 'seq')), parts along dimension 0, may hold values from -6 to 6
- decode_q: bfloat16 [32, 4096], P(('groups', 'seq')), parts along dimension 0, may hold values from -128 to 128
- decode_k: bfloat16 [32, 256, 1024], P(('groups', 'seq')), parts along dimension 0, may hold values from -6 to 6
- decode_v: bfloat16 [32, 256, 1024], P(('groups', 'seq')), parts along dimension 0, may hold values from -6 to 6
- decode_len: int32 [32], P(('groups', 'seq')), parts along dimension 0, may hold values from 2 to 256, as said below
- expert_idx: int32 [160, 2], P(('groups', 'seq')), parts along dimension 0, may hold values from 0 to 3, all different within a row; in each aligned block of 5 rows (0 to 4, 5 to 9, ...) at most 4 rows name the same one
- gate_w: float32 [160, 2], P(('groups', 'seq')), parts along dimension 0, may hold values from 0.2 to 1
- norm_gain: float32 [4096], replicated, may hold values from 0.1 to 1.9
- w_gate: bfloat16 [16, 4096, 1792], P('seq'), may hold values from -0.09375 to 0.09375
- w_up: bfloat16 [16, 4096, 1792], P('seq'), may hold values from -0.09375 to 0.09375
- w_down: bfloat16 [16, 1792, 4096], P('seq'), may hold values from -0.0625 to 0.0625
Outputs:
- prefill_out: bfloat16 [128, 4096], P(('groups', 'seq')), parts along dimension 0
- decode_out: bfloat16 [32, 4096], P(('groups', 'seq')), parts along dimension 0
The draws below stay inside these ranges and needn't reach their ends.
There are 2 independent parts, one for each index of `groups`. The reference program is written for one: setup_inputs(seed, part) draws one part's arguments, and reference() takes and returns one part's arrays. A program takes and returns all parts, laid end to end along the dimension named above; an argument that names none is the same for every part. Nothing has to cross between parts.
Inputs may be any that keep to these rules, and one draw needn't show every extreme that they name: `expert_idx`: within the 5 rows of one device the 2 experts of a row differ and no expert is named by more than 4 rows; some expert is named by exactly 4 rows of one device. `decode_len`: some row has 256 live positions.
All inputs are finite; a program needn't handle non-finite values.
Results may differ from the reference program's by a relative error of at most 0.019.
Values may be sent and summed in bfloat16 or wider, within the bound.
A program may use at most 128 MiB of HBM per device.

```python
import math
import jax
import jax.numpy as jnp
import numpy as np
from jax import lax

D = 4096
HEADS = 32
KV_HEADS = 8
HEAD = 128
EXPERTS = 4
TOP = 2
FF = 7168
Q_DEV = 4
DEC_DEV = 1
DEC_LEN = 256
ROWS_DEV = 5
CAP = 4
SLICES = 4
FF_DEV = 1792
PRE_TOK = 64
CTX = 4096
DEC_ROWS = 16
ROWS = 80
N_SEQ = 16


def draw_prefill_q(key, part):
    inner = jax.random.fold_in(key, 11)
    return jnp.clip(3.0 * jax.random.normal(inner, (PRE_TOK, HEADS * HEAD), jnp.float32), -12.0, 12.0).astype(jnp.bfloat16)


def draw_decode_q(key, part):
    inner = jax.random.fold_in(key, 13)
    return jnp.clip(3.0 * jax.random.normal(inner, (DEC_ROWS, HEADS * HEAD), jnp.float32), -12.0, 12.0).astype(jnp.bfloat16)


def draw_prefill_k(key, part):
    inner = jax.random.fold_in(key, 17)
    return jnp.clip(jax.random.normal(inner, (CTX, KV_HEADS * HEAD), jnp.float32), -6.0, 6.0).astype(jnp.bfloat16)


def draw_decode_k(key, part):
    inner = jax.random.fold_in(key, 19)
    return jnp.clip(jax.random.normal(inner, (DEC_ROWS, DEC_LEN, KV_HEADS * HEAD), jnp.float32), -6.0, 6.0).astype(jnp.bfloat16)


def draw_decode_len(key, part):
    lengths = jax.random.randint(jax.random.fold_in(key, 23), (DEC_ROWS,), 2, DEC_LEN + 1)
    return lengths.at[0].set(DEC_LEN).astype(jnp.int32)


def shard_levels(stream_key, dims, split, smallest, high):
    gain, own = 1.0, jax.random.fold_in(stream_key, 6)
    for axis_at, shards_of in split:
        draws = jnp.exp(jax.random.uniform(jax.random.fold_in(own, axis_at), (shards_of,), jnp.float32, smallest / len(split), high / len(split)))
        gain = gain * jnp.repeat(draws, dims[axis_at] // shards_of).reshape([-1 if axis == axis_at else 1 for axis in range(len(dims))])
    return gain


def shared_out(key, own, number, rows, number_of, top, most, slope):
    order = jax.random.permutation(key, number_of)
    crowded, common = load_shares(number_of, rows * top, most, slope, True), load_shares(number_of, rows * top, most, slope, False)
    places = jnp.arange(number_of)

    def named(tallies, offset_by):
        used = int((tallies > 0).sum())
        fixed = max(1, used // 4)
        shifted = fixed + (places - fixed + offset_by * (used - fixed)) % max(1, number_of - fixed)
        return jnp.zeros((number_of,), jnp.int32).at[order[jnp.where(places < fixed, places, shifted)]].set(jnp.asarray(tallies, jnp.int32))

    tallies = jnp.where(number % 4 == 0, named(crowded, number // 4), named(common, number - number // 4 - 1))
    mixed = jax.random.permutation(jax.random.fold_in(own, 3), number_of)
    giver, receiver = mixed[0:number_of // 2 * 2:2], mixed[1:number_of // 2 * 2:2]
    slack = jnp.minimum(tallies[giver] - 1, most - tallies[receiver]) // 2
    slack = jnp.where((giver == order[0]) | (receiver == order[0]) | (tallies[receiver] == 0), 0, jnp.maximum(slack, 0))
    shifted = jax.random.randint(jax.random.fold_in(own, 4), (number_of // 2,), 0, 1 << 20) % (slack + 1)
    tallies = tallies.at[giver].add(-shifted).at[receiver].add(shifted)
    items = jnp.searchsorted(jnp.cumsum(tallies), jnp.arange(rows * top), side="right").astype(jnp.int32)
    table = items.reshape(top, rows).T
    table = table[jax.random.permutation(jax.random.fold_in(own, 1), rows)]
    offset_by = jax.random.randint(jax.random.fold_in(own, 2), (rows, 1), 0, top)
    return jnp.take_along_axis(table, (jnp.arange(top)[None, :] + offset_by) % top, axis=1)


def load_shares(amount, total, limit, skew, full):
    loads = [(1 << 20) // math.isqrt(grade ** skew) + 1 for grade in range(1, amount + 1)]
    largest = limit if full else min(limit, max(-(-total // amount), total * loads[0] // sum(loads)))
    least = 1 if total - largest >= amount - 1 else 0
    counts, rest = [largest] + [least] * (amount - 1), total - largest - least * (amount - 1)
    while rest > 0:
        free = [i for i in range(1, amount) if counts[i] < largest] or [i for i in range(1, amount) if counts[i] < limit]
        pool, left = sum([loads[i] for i in free]), rest
        for i in free:
            addition = min(limit - counts[i], max(1, left * loads[i] // pool), rest)
            counts[i] = counts[i] + addition
            rest = rest - addition
    return np.array(counts)


def scatter_about(own_key, extent, scale, limit, cuts=(), kind=jnp.bfloat16):
    factor_of = shard_levels(own_key, extent, cuts, -0.22, 0.18) if cuts else 1.0
    drawn = jax.random.normal(own_key, extent, jnp.float32) * scale * factor_of
    return jnp.minimum(jnp.maximum(drawn, -limit), limit).astype(kind)


def setup_inputs(seed: int = 0, part: int = 0) -> dict:
    arg_keys = jax.random.split(jax.random.key(seed), 14)
    part_splits = jax.random.split(jax.random.fold_in(arg_keys[13], part), 14)
    prefill_q = draw_prefill_q(jax.random.fold_in(jax.random.fold_in(arg_keys[13], part), 71), part)
    prefill_k = draw_prefill_k(jax.random.fold_in(jax.random.fold_in(arg_keys[13], part), 71), part)
    prefill_v = scatter_about(part_splits[2], (CTX, KV_HEADS * HEAD), 1.0, 6.0, ((0, 16),))
    decode_q = draw_decode_q(jax.random.fold_in(jax.random.fold_in(arg_keys[13], part), 71), part)
    decode_k = draw_decode_k(jax.random.fold_in(jax.random.fold_in(arg_keys[13], part), 71), part)
    decode_v = scatter_about(part_splits[5], (DEC_ROWS, DEC_LEN, KV_HEADS * HEAD), 1.0, 6.0, ((0, 16),))
    decode_len = draw_decode_len(jax.random.fold_in(jax.random.fold_in(arg_keys[13], part), 71), part)
    expert_idx_keys = jax.random.split(jax.random.fold_in(part_splits[7], 1), ROWS // ROWS_DEV)
    expert_idx_turns = jax.random.permutation(jax.random.fold_in(part_splits[7], 3), ROWS // ROWS_DEV)
    expert_idx = jax.vmap(lambda own, number: shared_out(jax.random.fold_in(part_splits[7], 2), own, number, ROWS_DEV, EXPERTS, TOP, CAP, 2))(expert_idx_keys, expert_idx_turns).reshape((ROWS, TOP))
    gate_w = jnp.clip(0.2 + 0.8 * jax.random.uniform(part_splits[8], (ROWS, TOP), jnp.float32) ** shard_levels(part_splits[8], (ROWS, TOP), ((0, 16),), -0.2, 0.2), 0.2, 1.0)
    norm_gain = jnp.clip(1.0 + 0.18 * jax.random.normal(arg_keys[9], (D,), jnp.float32), 0.1, 1.9)
    w_gate = scatter_about(arg_keys[10], (EXPERTS * SLICES, D, FF_DEV), D ** -0.5, 0.09375, ((0, 16),))
    w_up = scatter_about(arg_keys[11], (EXPERTS * SLICES, D, FF_DEV), D ** -0.5, 0.09375, ((0, 16),))
    w_down = scatter_about(arg_keys[12], (EXPERTS * SLICES, FF_DEV, D), FF ** -0.5, 0.0625, ((0, 16),))
    return {"prefill_q": prefill_q, "prefill_k": prefill_k, "prefill_v": prefill_v, "decode_q": decode_q, "decode_k": decode_k, "decode_v": decode_v, "decode_len": decode_len, "expert_idx": expert_idx, "gate_w": gate_w, "norm_gain": norm_gain, "w_gate": w_gate, "w_up": w_up, "w_down": w_down}


def prefill_attention(prefill_q, prefill_k, prefill_v):
    members = HEADS // KV_HEADS
    keyed = prefill_k.astype(jnp.float32).reshape(CTX, KV_HEADS, HEAD)
    valued = prefill_v.astype(jnp.float32).reshape(CTX, KV_HEADS, HEAD)

    def one_block(block):
        grouped = block.astype(jnp.float32).reshape(Q_DEV, KV_HEADS, members, HEAD)
        scores = jnp.einsum('rhgc,khc->rhgk', grouped, keyed, precision=lax.Precision.HIGHEST) * HEAD ** (-0.5)
        peaks = lax.optimization_barrier(jnp.max(scores, axis=-1, keepdims=True))
        weights = jnp.exp(scores - peaks)
        totals = lax.optimization_barrier(jnp.sum(weights, axis=-1))
        rounded = lax.optimization_barrier(weights.astype(jnp.bfloat16))
        output = jnp.einsum('rhgk,khc->rhgc', rounded.astype(jnp.float32), valued, precision=lax.Precision.HIGHEST)
        output = output / totals[..., None]
        return output.reshape(Q_DEV, HEADS * HEAD).astype(jnp.bfloat16)
    return lax.map(one_block, prefill_q.reshape(N_SEQ, Q_DEV, HEADS * HEAD))

def decode_attention(decode_q, decode_k, decode_v, decode_len):
    members = HEADS // KV_HEADS
    grouped = decode_q.astype(jnp.float32).reshape(DEC_ROWS, KV_HEADS, members, HEAD)
    keyed = decode_k.astype(jnp.float32).reshape(DEC_ROWS, DEC_LEN, KV_HEADS, HEAD)
    valued = decode_v.astype(jnp.float32).reshape(DEC_ROWS, DEC_LEN, KV_HEADS, HEAD)
    scores = jnp.einsum('bhgc,blhc->bhgl', grouped, keyed, precision=lax.Precision.HIGHEST) * HEAD ** (-0.5)
    live = jnp.arange(DEC_LEN, dtype=jnp.int32)[None, :] < decode_len[:, None]
    live = live[:, None, None, :]
    scores = jnp.where(live, scores, -1e+30)
    peaks = lax.optimization_barrier(jnp.max(scores, axis=-1, keepdims=True))
    weights = jnp.where(live, jnp.exp(scores - peaks), 0.0)
    totals = lax.optimization_barrier(jnp.sum(weights, axis=-1))
    rounded = lax.optimization_barrier(weights.astype(jnp.bfloat16))
    output = jnp.einsum('bhgl,blhc->bhgc', rounded.astype(jnp.float32), valued, precision=lax.Precision.HIGHEST)
    output = output / totals[..., None]
    return output.reshape(DEC_ROWS, HEADS * HEAD).astype(jnp.bfloat16)

def expert_outputs(normed, w_gate, w_up, w_down):
    slices = N_SEQ // EXPERTS
    width = FF // slices
    gates = w_gate.reshape(EXPERTS, slices, D, width)
    raises = w_up.reshape(EXPERTS, slices, D, width)
    downs = w_down.reshape(EXPERTS, slices, width, D)
    widened = normed.astype(jnp.float32)

    def one_expert(weights):
        gate_part, up_part, down_part = weights
        gated = jnp.einsum('rd,sdf->rsf', widened, gate_part.astype(jnp.float32), precision=lax.Precision.HIGHEST)
        raised = jnp.einsum('rd,sdf->rsf', widened, up_part.astype(jnp.float32), precision=lax.Precision.HIGHEST)
        hidden = lax.optimization_barrier((jax.nn.silu(gated) * raised).astype(jnp.bfloat16))
        pieces = jnp.einsum('rsf,sfd->rsd', hidden.astype(jnp.float32), down_part.astype(jnp.float32), precision=lax.Precision.HIGHEST)
        rounded = lax.optimization_barrier(pieces.astype(jnp.bfloat16))
        return lax.optimization_barrier(jnp.sum(rounded.astype(jnp.float32), axis=1))
    return lax.map(one_expert, (gates, raises, downs))

def reference(prefill_q, prefill_k, prefill_v, decode_q, decode_k, decode_v, decode_len, expert_idx, gate_w, norm_gain, w_gate, w_up, w_down):
    prefill_rows = prefill_attention(prefill_q, prefill_k, prefill_v)
    decode_rows = decode_attention(decode_q, decode_k, decode_v, decode_len).reshape(N_SEQ, DEC_DEV, D)
    layer_in = jnp.concatenate([prefill_rows, decode_rows], axis=1).reshape(ROWS, D)
    widened = layer_in.astype(jnp.float32)
    mean_square = lax.optimization_barrier(jnp.mean(widened * widened, axis=-1, keepdims=True))
    normed = (widened * lax.rsqrt(mean_square + 1e-05) * norm_gain).astype(jnp.bfloat16)
    outputs = expert_outputs(normed, w_gate, w_up, w_down)
    positions = jnp.arange(ROWS, dtype=jnp.int32)
    mixed = widened
    for choose in range(TOP):
        mixed = mixed + gate_w[:, choose:choose + 1] * outputs[expert_idx[:, choose], positions]
    result = mixed.astype(jnp.bfloat16).reshape(N_SEQ, ROWS_DEV, D)
    return (result[:, :Q_DEV].reshape(PRE_TOK, D), result[:, Q_DEV:].reshape(DEC_ROWS, D))
```

```python
import functools

import jax
import jax.numpy as jnp
from jax import lax
from jax.experimental import pallas as pl
from jax.experimental.pallas import tpu as pltpu
from jax.sharding import PartitionSpec as P

HEADS = 32
KV = 8
MEM = HEADS // KV
HEAD = 128
EXPERTS = 4
CAP = 4
HALF = KV // 2
F32 = jnp.float32
BF = jnp.bfloat16
CHUNKS = 4
MESH = pl.DeviceIdType.MESH


def body(
    n,
    q_hbm,
    dq_hbm,
    len_ref,
    idx_ref,
    gate_ref,
    gain_hbm,
    k_hbm,
    v_hbm,
    dk_hbm,
    dv_hbm,
    wg_hbm,
    wu_hbm,
    wd_hbm,
    out_ref,
    q_ref,
    dq_ref,
    gain_ref,
    k_ref,
    v_ref,
    dk_ref,
    dv_ref,
    wg_ref,
    wu_ref,
    wd_ref,
    qs,
    qp,
    qb,
    qg,
    sb,
    rb,
    dqs,
    gs,
    xl,
    ss,
    iv,
    pm,
    gm,
    xs,
    xg,
    xf,
    x,
    hid,
    pf,
    pb,
    p1,
    ys,
    yr,
    osc,
    gsend,
    grecv,
    rsend,
    rrecv,
    psend,
    precv,
    ysend,
    yrecv,
    local,
):
    hs = n // (2 * EXPERTS)
    nc = hs * EXPERTS
    me = lax.axis_index("seq")
    core = lax.rem(me, 2)
    h = lax.rem(me // 2, hs)
    outer = me // (2 * hs)
    other = 1 - core

    def at(o, hh, c):
        return {"seq": (o * hs + hh) * 2 + c}

    def there(j, d, c):
        return at(lax.rem(outer + d, EXPERTS), lax.rem(h + j, hs), c)

    def slot_to(j, d):
        return lax.rem(h + j, hs) * EXPERTS + lax.rem(outer + d, EXPERTS)

    def slot_from(j, d):
        return lax.rem(h + hs - j, hs) * EXPERTS + lax.rem(outer + EXPERTS - d, EXPERTS)

    partner = at(outer, h, other)
    mine = h * EXPERTS + outer
    chips = [(j, d) for j in range(hs) for d in range(EXPERTS)]
    barrier = pltpu.get_barrier_semaphore()
    for j, d in chips:
        for c in (core, other):
            if (j, d) != (0, 0) or c is other:
                pl.semaphore_signal(barrier, inc=1, device_id=there(j, d, c), device_id_type=MESH)

    length = k_ref.shape[0] // 2
    cols = HALF * HEAD

    def half(c):
        return pl.ds(pl.multiple_of(c * cols, cols), cols)

    sources = [
        (q_hbm, q_ref),
        (dq_hbm, dq_ref),
        (gain_hbm, gain_ref),
        (dk_hbm.at[0], dk_ref),
        (dv_hbm.at[0], dv_ref),
        (k_hbm.at[:, half(core)], k_ref.at[pl.ds(0, length)]),
        (v_hbm.at[:, half(core)], v_ref.at[pl.ds(0, length)]),
        (wg_hbm.at[0], wg_ref),
        (wu_hbm.at[0], wu_ref),
        (wd_hbm.at[0], wd_ref),
    ]
    loads = [pltpu.make_async_copy(s, t, local.at[i]) for i, (s, t) in enumerate(sources)]
    for load in loads[:7]:
        load.start()

    def remote(src, dst, ssem, rsem, peer):
        return pltpu.make_async_remote_copy(
            src_ref=src, dst_ref=dst, send_sem=ssem, recv_sem=rsem,
            device_id=peer, device_id_type=MESH,
        )

    tokens = q_ref.shape[0]
    rows = tokens + 1
    mt = MEM * tokens
    bs = MEM * CAP
    lanes = [slice(c * HEAD, (c + 1) * HEAD) for c in range(KV)]

    loads[0].wait()
    wide = q_ref[...].astype(F32)
    for c in range(KV):
        for m in range(MEM):
            i = c * MEM + m
            qs[c, m * tokens : (m + 1) * tokens, :] = wide[:, i * HEAD : (i + 1) * HEAD]
    qp[...] = qs[pl.ds(other * HALF, HALF)].astype(BF)
    qb[:, pl.ds(pl.multiple_of(core * mt, mt), mt), :] = qs[pl.ds(core * HALF, HALF)].astype(BF)

    pl.semaphore_wait(barrier, n - 1)
    early = [
        remote(qp, qb.at[:, pl.ds(pl.multiple_of(core * mt, mt), mt)], psend.at[0], precv.at[0], partner),
        remote(k_hbm.at[:, half(other)], k_ref.at[pl.ds(length, length)], psend.at[1], precv.at[1], partner),
        remote(v_hbm.at[:, half(other)], v_ref.at[pl.ds(length, length)], psend.at[2], precv.at[2], partner),
    ]
    for copy in early:
        copy.start()
    for load in loads[7:]:
        load.start()

    def gather_start(phase, src_of, dst):
        sent = {}
        order = sorted(chips[1:], key=lambda jd: -min(jd[1], EXPERTS - jd[1]))
        for j, d in order:
            copy = remote(
                src_of(d), dst, gsend.at[phase, j * EXPERTS + d], grecv.at[phase, j * EXPERTS + d],
                there(j, d, core),
            )
            copy.start()
            sent[j, d] = copy
        return sent

    qrows = 2 * mt

    def qslot(slot, count=1):
        return pl.ds(pl.multiple_of(slot * qrows, qrows), count * qrows)

    early[0].wait_recv()
    sent = gather_start(0, lambda d: qb, qg.at[:, qslot(mine)])
    qg[:, qslot(mine), :] = qb[...]

    spots = []
    for r in range(rows):
        for t in range(idx_ref.shape[0]):
            named = idx_ref[t, r]
            spot = jnp.int32(0)
            for before in range(r):
                hit = (idx_ref[0, before] == named) | (idx_ref[1, before] == named)
                spot = spot + jnp.where(hit, 1, 0)
            spots.append((r, named, spot, gate_ref[t, r]))

    def token_of(i):
        return jnp.where(i < mt, lax.rem(i, tokens), jnp.where(i < mt + MEM, tokens, rows))

    def member_of(i):
        return jnp.where(i < mt, i // tokens, i - mt)

    side = xl.shape[0]
    a = lax.broadcasted_iota(jnp.int32, (EXPERTS * bs, side), 0)
    b = lax.broadcasted_iota(jnp.int32, (EXPERTS * bs, side), 1)
    same = lax.rem(a, bs) // CAP == member_of(b)
    pick = jnp.zeros((EXPERTS * bs, side), F32)
    code = a // bs * CAP + lax.rem(a, CAP)
    tok = jnp.where(same, token_of(b), rows)
    for r, named, spot, _ in spots:
        pick = jnp.where((tok == r) & (code == named * CAP + spot), 1.0, pick)
    pm[...] = pick.astype(BF)
    a = lax.broadcasted_iota(jnp.int32, (side, nc * bs), 0)
    b = lax.broadcasted_iota(jnp.int32, (side, nc * bs), 1)
    same = lax.rem(b, bs) // CAP == member_of(a)
    tok = jnp.where(same, token_of(a), rows)
    expert = lax.rem(outer + EXPERTS - lax.rem(b // bs, EXPERTS), EXPERTS)
    code = expert * CAP + lax.rem(b, CAP)
    mix = jnp.zeros((side, nc * bs), F32)
    for r, named, spot, gate in spots:
        mix = jnp.where((tok == r) & (code == named * CAP + spot), gate, mix)
    high = mix.astype(BF)
    gm[0] = high
    gm[1] = (mix - high.astype(F32)).astype(BF)

    scale = HEAD ** (-0.5)
    xl[...] = jnp.zeros(xl.shape, F32)
    iv[...] = jnp.zeros(iv.shape, F32)
    gs[...] = jnp.zeros(gs.shape, F32)
    loads[1].wait()
    loads[2].wait()
    wide = dq_ref[...].astype(F32)
    for c in range(KV):
        for m in range(MEM):
            i = c * MEM + m
            gain = gain_ref[:, i * HEAD : (i + 1) * HEAD]
            dqs[i : i + 1, :] = wide[:, i * HEAD : (i + 1) * HEAD]
            gs[m * tokens : (m + 1) * tokens, lanes[c]] = jnp.broadcast_to(gain, (tokens, HEAD))
            gs[mt + m : mt + m + 1, lanes[c]] = gain
    dq = dqs[...].astype(BF)
    dlen = dk_ref.shape[0]
    loads[3].wait()
    head_of = lax.broadcasted_iota(jnp.int32, (HEADS, dlen), 0) // MEM
    scores = jnp.zeros((HEADS, dlen), F32)
    for c in range(KV):
        part = lax.dot_general(
            dq, dk_ref[:, lanes[c]], (((1,), (1,)), ((), ())), preferred_element_type=F32
        )
        scores = jnp.where(head_of == c, part, scores)
    scores = scores * scale
    live = lax.broadcasted_iota(jnp.int32, (HEADS, dlen), 1) < len_ref[0]
    scores = jnp.where(live, scores, -1e30)
    peak = jnp.max(scores, axis=-1, keepdims=True)
    weights = jnp.where(live, jnp.exp(scores - peak), 0.0)
    total = jnp.sum(weights, axis=-1, keepdims=True)
    loads[4].wait()
    acc = jnp.zeros((HEADS, HEAD), F32)
    for c in range(KV):
        masked = jnp.where(head_of == c, weights, 0.0).astype(BF)
        acc = acc + jnp.dot(masked, dv_ref[:, lanes[c]], preferred_element_type=F32)
    dqs[...] = (acc / total).astype(BF).astype(F32)
    for c in range(KV):
        xl[mt : mt + MEM, lanes[c]] = dqs[c * MEM : (c + 1) * MEM, :]

    loads[5].wait()
    loads[6].wait()
    early[1].wait_recv()
    early[2].wait_recv()
    returns = []
    count = EXPERTS * qrows
    lane = lax.broadcasted_iota(jnp.int32, (count, HEAD), 1)
    for j in range(hs):
        for d in range(EXPERTS):
            if (j, d) != (0, 0):
                sent[j, d].wait_recv()
        group = lax.rem(h + hs - j, hs)
        stats = jnp.zeros((count, HEAD), F32)
        first = pl.multiple_of(group * EXPERTS * 2, EXPERTS * 2)
        for c in range(HALF):
            sc = lax.dot_general(
                qg[c, qslot(group * EXPERTS, EXPERTS), :], k_ref[:, lanes[c]],
                (((1,), (1,)), ((), ())), preferred_element_type=F32,
            ) * scale
            pk = jnp.max(sc, axis=-1, keepdims=True).astype(BF).astype(F32)
            w = jnp.exp(sc - pk)
            tot = jnp.sum(w, axis=-1, keepdims=True)
            num = jnp.dot(w.astype(BF), v_ref[:, lanes[c]], preferred_element_type=F32)
            sb[pl.ds(first, EXPERTS * 2), c] = num.astype(BF).reshape(EXPERTS * 2, mt, HEAD)
            tot_high = tot.astype(BF).astype(F32)
            stats = jnp.where(lane == c, pk, stats)
            stats = jnp.where(lane == HALF + c, tot_high, stats)
            stats = jnp.where(lane == 2 * HALF + c, tot - tot_high, stats)
        sb[pl.ds(first, EXPERTS * 2), HALF] = stats.astype(BF).reshape(EXPERTS * 2, mt, HEAD)
        order = sorted(range(EXPERTS), key=lambda d: -min(d, EXPERTS - d))
        for d in order:
            for rc in range(2):
                to = core if rc == 0 else other
                src = sb.at[slot_to((hs - j) % hs, d) * 2 + to]
                i = (((hs - j) % hs) * EXPERTS + d) * 2 + rc
                if i == 0:
                    copy = pltpu.make_async_copy(src, rb.at[0], rrecv.at[0])
                else:
                    copy = remote(
                        src, rb.at[i], rsend.at[i], rrecv.at[i], there((hs - j) % hs, d, to)
                    )
                copy.start()
                returns.append((i, copy))
    returns.sort(key=lambda e: e[0])

    for rc in range(2):
        found = [i for i in range(rc, 2 * nc, 2)]
        for i in found:
            if i == 0:
                returns[i][1].wait()
            else:
                returns[i][1].wait_recv()
        stat = [rb[i, HALF].astype(F32) for i in found]
        top = functools.reduce(jnp.maximum, stat)
        part = [jnp.exp(jnp.minimum(s - top, 0.0)) for s in stat]
        den = jnp.zeros((mt, HEAD), F32)
        for s, f in zip(stat, part):
            den = den + f * (
                pltpu.roll(s, HEAD - HALF, 1) + pltpu.roll(s, HEAD - 2 * HALF, 1)
            )
        ln = lax.broadcasted_iota(jnp.int32, (mt, HEAD), 1)
        inverse = 1.0 / jnp.where(ln < HALF, den, 1.0)
        part = [f * inverse for f in part]
        source = core if rc == 0 else other
        for c in range(HALF):
            acc = jnp.zeros((mt, HEAD), F32)
            for i, f in zip(found, part):
                acc = acc + rb[i, c].astype(F32) * f[:, c : c + 1]
            xl[0:mt, pl.ds(pl.multiple_of(source * cols + c * HEAD, HEAD), HEAD)] = acc.astype(
                BF
            ).astype(F32)

    layer = xl[...]
    ss[...] = jnp.broadcast_to(
        jnp.sum(layer * layer, axis=1, keepdims=True) / (HEADS * HEAD), ss.shape
    )
    pre = ss[0:tokens, :]
    dec = ss[mt : mt + 1, :]
    for m in range(1, MEM):
        pre = pre + ss[m * tokens : (m + 1) * tokens, :]
        dec = dec + ss[mt + m : mt + m + 1, :]
    pre = lax.rsqrt(pre + 1e-05)
    for m in range(MEM):
        iv[m * tokens : (m + 1) * tokens, :] = pre
    iv[mt : mt + MEM, :] = jnp.broadcast_to(lax.rsqrt(dec + 1e-05), (MEM, HEAD))
    inv = iv[...]
    normed = jnp.concatenate([layer[:, s] * inv * gs[:, s] for s in lanes], axis=1).astype(BF)
    xs[...] = (
        jnp.dot(pm[...], normed, preferred_element_type=F32).astype(BF).reshape(EXPERTS, bs, -1)
    )

    def xrow(slot, c):
        return pl.ds(pl.multiple_of((c * nc + slot) * bs, bs), bs)

    moved = gather_start(
        1, lambda d: xs.at[lax.rem(outer + d, EXPERTS)], xg.at[xrow(mine, core)]
    )
    own = remote(xs.at[outer], xg.at[xrow(mine, core)], psend.at[3], precv.at[3], partner)
    own.start()
    shared = [own]

    def widen(where):
        for c in range(KV):
            xf[c, where, :] = xg[where, lanes[c]].astype(F32)

    xg[xrow(mine, core), :] = xs[outer]
    widen(xrow(mine, core))
    arrival = sorted(chips[1:], key=lambda jd: (min(jd[1], EXPERTS - jd[1]) + (jd[0] > 0)))
    for j, d in arrival:
        moved[j, d].wait_recv()
        where = xrow(slot_from(j, d), core)
        i = j * EXPERTS + d
        copy = remote(xg.at[where], xg.at[where], psend.at[3 + i], precv.at[3 + i], partner)
        copy.start()
        shared.append(copy)
        widen(where)
    for copy, (j, d) in zip(shared, [(0, 0)] + arrival):
        copy.wait_recv()
        widen(xrow(slot_from(j, d), other))
    for k in range(CAP):
        for c in range(KV):
            for m in range(MEM):
                i = c * MEM + m
                x[k * n : (k + 1) * n, i * HEAD : (i + 1) * HEAD] = xf[
                    c, pl.ds(m * CAP + k, n, stride=bs), :
                ].astype(BF)

    for load in loads[7:]:
        load.wait()
    ff = wg_ref.shape[1]
    step = 256 if ff % 256 == 0 else ff

    def up(i, carry):
        where = pl.ds(pl.multiple_of(i * step, step), step) if step != ff else slice(None)
        gated = jnp.dot(x[...], wg_ref[:, where], preferred_element_type=F32)
        raised = jnp.dot(x[...], wu_ref[:, where], preferred_element_type=F32)
        hid[:, where] = (gated / (1.0 + jnp.exp(-gated)) * raised).astype(BF)
        return carry

    lax.fori_loop(0, ff // step, up, 0)

    each = KV // CHUNKS
    width = each * HEAD
    far = nc * bs
    swaps = []
    for g in range(CHUNKS):
        for e in range(each):
            c = g * each + e
            piece = jnp.dot(
                hid[...], wd_ref[:, c * MEM * HEAD : (c + 1) * MEM * HEAD], preferred_element_type=F32
            ).astype(BF).astype(F32)
            for k in range(CAP):
                for m in range(MEM):
                    pf[c, pl.ds(m * CAP + k, n, stride=bs), :] = piece[k * n : (k + 1) * n, lanes[m]]
            pb[g, :, lanes[e]] = pf[c, pl.ds(pl.multiple_of(other * far, far), far), :].astype(BF)
        i = 3 + nc + g
        copy = remote(pb.at[g], p1.at[g], psend.at[i], precv.at[i], partner)
        copy.start()
        swaps.append(copy)
    outs = []
    order = sorted(chips[1:], key=lambda jd: -(min(jd[1], EXPERTS - jd[1]) + (jd[0] > 0)))
    for g in range(CHUNKS):
        swaps[g].wait_recv()
        for e in range(each):
            c = g * each + e
            ys[g, :, lanes[e]] = (
                pf[c, pl.ds(pl.multiple_of(core * far, far), far), :]
                + p1[g, :, lanes[e]].astype(F32)
            ).astype(BF)
        for j, d in order:
            i = j * EXPERTS + d
            copy = remote(
                ys.at[g, pl.ds(pl.multiple_of(slot_to(j, d) * bs, bs), bs)],
                yr.at[g, pl.ds(i * bs, bs)],
                ysend.at[g, i], yrecv.at[g, i], there(j, d, core),
            )
            copy.start()
            outs.append(copy)
        yr[g, 0:bs, :] = ys[g, pl.ds(pl.multiple_of(mine * bs, bs), bs), :]
    each_out = len(order)
    for g in range(CHUNKS):
        for copy in outs[g * each_out : (g + 1) * each_out]:
            copy.wait_recv()
        where = slice(g * width, (g + 1) * width)
        osc[:, where] = (
            xl[:, where]
            + jnp.dot(gm[0], yr[g], preferred_element_type=F32)
            + jnp.dot(gm[1], yr[g], preferred_element_type=F32)
        )
    for c in range(KV):
        for m in range(MEM):
            i = c * MEM + m
            out_ref[0:tokens, i * HEAD : (i + 1) * HEAD] = osc[
                m * tokens : (m + 1) * tokens, lanes[c]
            ]
            out_ref[tokens:rows, i * HEAD : (i + 1) * HEAD] = osc[mt + m : mt + m + 1, lanes[c]]
    for copy in early + list(sent.values()) + list(moved.values()) + shared + swaps + outs:
        copy.wait_send()
    for i, copy in returns:
        if i:
            copy.wait_send()


def on_device(n, *args):
    (q, k, v, dq, dk, dv, dlen, idx, gate, gain, wg, wu, wd) = args
    width = q.shape[1]
    tokens = q.shape[0]
    rows = tokens + dq.shape[0]
    nc = n // 2
    ff = wg.shape[2]
    mt, bs = MEM * tokens, MEM * CAP
    side = (mt + MEM + 15) // 16 * 16
    lanes = KV * HEAD
    hbm = pl.BlockSpec(memory_space=pl.ANY)
    vm = pl.BlockSpec(memory_space=pltpu.VMEM)
    sm = pl.BlockSpec(memory_space=pltpu.SMEM)
    positions = 2 * k.shape[0]
    dma = pltpu.SemaphoreType.DMA
    out = pl.pallas_call(
        functools.partial(body, n),
        out_shape=jax.ShapeDtypeStruct((rows, width), F32),
        in_specs=[hbm, hbm, sm, sm, sm, hbm] + [hbm] * 7,
        out_specs=vm,
        scratch_shapes=[
            pltpu.VMEM(q.shape, BF),
            pltpu.VMEM(dq.shape, BF),
            pltpu.VMEM((1, width), F32),
            pltpu.VMEM((positions, HALF * HEAD), BF),
            pltpu.VMEM((positions, HALF * HEAD), BF),
            pltpu.VMEM(dk.shape[1:], BF),
            pltpu.VMEM(dv.shape[1:], BF),
            pltpu.VMEM(wg.shape[1:], BF),
            pltpu.VMEM(wu.shape[1:], BF),
            pltpu.VMEM(wd.shape[1:], BF),
            pltpu.VMEM((KV, mt, HEAD), F32),
            pltpu.VMEM((HALF, mt, HEAD), BF),
            pltpu.VMEM((HALF, 2 * mt, HEAD), BF),
            pltpu.VMEM((HALF, nc * 2 * mt, HEAD), BF),
            pltpu.VMEM((n, HALF + 1, mt, HEAD), BF),
            pltpu.VMEM((n, HALF + 1, mt, HEAD), BF),
            pltpu.VMEM((HEADS, HEAD), F32),
            pltpu.VMEM((side, lanes), F32),
            pltpu.VMEM((side, lanes), F32),
            pltpu.VMEM((side, HEAD), F32),
            pltpu.VMEM((side, HEAD), F32),
            pltpu.VMEM((EXPERTS * bs, side), BF),
            pltpu.VMEM((2, side, nc * bs), BF),
            pltpu.VMEM((EXPERTS, bs, lanes), BF),
            pltpu.VMEM((n * bs, lanes), BF),
            pltpu.VMEM((KV, n * bs, HEAD), F32),
            pltpu.VMEM((n * CAP, width), BF),
            pltpu.VMEM((n * CAP, ff), BF),
            pltpu.VMEM((KV, n * bs, HEAD), F32),
            pltpu.VMEM((CHUNKS, nc * bs, lanes // CHUNKS), BF),
            pltpu.VMEM((CHUNKS, nc * bs, lanes // CHUNKS), BF),
            pltpu.VMEM((CHUNKS, nc * bs, lanes // CHUNKS), BF),
            pltpu.VMEM((CHUNKS, nc * bs, lanes // CHUNKS), BF),
            pltpu.VMEM((side, lanes), F32),
            dma((2, nc)),
            dma((2, nc)),
            dma((2 * nc,)),
            dma((2 * nc,)),
            dma((3 + nc + CHUNKS,)),
            dma((3 + nc + CHUNKS,)),
            dma((CHUNKS, nc)),
            dma((CHUNKS, nc)),
            dma((10,)),
        ],
        compiler_params=pltpu.CompilerParams(
            collective_id=0, has_side_effects=True, vmem_limit_bytes=60_000_000
        ),
        name="moe_layer",
    )(q, dq, dlen, idx.T, gate.T, gain[None], k, v, dk, dv, wg, wu, wd)
    return out[:tokens].astype(BF), out[tokens:].astype(BF)


def solution(mesh):
    both = ("groups", "seq")
    in_specs = (
        P(both, None),
        P(both, None),
        P(both, None),
        P(both, None),
        P(both, None, None),
        P(both, None, None),
        P(both),
        P(both, None),
        P(both, None),
        P(),
        P("seq", None, None),
        P("seq", None, None),
        P("seq", None, None),
    )
    return jax.shard_map(
        functools.partial(on_device, mesh.shape["seq"]),
        mesh=mesh,
        in_specs=in_specs,
        out_specs=(P(both, None), P(both, None)),
        check_vma=False,
    )
```

```python
import functools

import jax
import jax.numpy as jnp
from jax import lax
from jax.experimental import pallas as pl
from jax.experimental.pallas import tpu as pltpu
from jax.sharding import PartitionSpec as P

HEADS = 32
KV = 8
MEM = HEADS // KV
HEAD = 128
EXPERTS = 4
CAP = 4
HALF = KV // 2
F32 = jnp.float32
BF = jnp.bfloat16
CHUNKS = 4
PARTS = 2
MESH = pl.DeviceIdType.MESH


def body(
    n,
    q_hbm,
    dq_hbm,
    len_hbm,
    idx_hbm,
    gate_hbm,
    gain_hbm,
    k_hbm,
    v_hbm,
    dk_hbm,
    dv_hbm,
    wg_hbm,
    wu_hbm,
    wd_hbm,
    out_ref,
    len_ref,
    idx_ref,
    gate_ref,
    q_ref,
    dq_ref,
    gain_ref,
    k_ref,
    v_ref,
    dk_ref,
    dv_ref,
    wg_ref,
    wu_ref,
    wd_ref,
    qs,
    qh,
    qg,
    sb,
    rb,
    st,
    rt,
    tr,
    dqs,
    gs,
    xl,
    ss,
    iv,
    pm,
    gm,
    xs,
    xg,
    xf,
    x,
    ga,
    ua,
    hid,
    pf,
    pb,
    p1,
    ys,
    yr,
    osc,
    qsend,
    qrecv,
    gsend,
    grecv,
    rsend,
    rrecv,
    tsend,
    trecv,
    psend,
    precv,
    ysend,
    yrecv,
    local,
):
    hs = n // (2 * EXPERTS)
    nc = hs * EXPERTS
    me = lax.axis_index("seq")
    core = lax.rem(me, 2)
    h = lax.rem(me // 2, hs)
    outer = me // (2 * hs)
    other = 1 - core

    def at(o, hh, c):
        return {"seq": (o * hs + hh) * 2 + c}

    def there(j, d, c):
        return at(lax.rem(outer + d, EXPERTS), lax.rem(h + j, hs), c)

    def slot_to(j, d):
        return lax.rem(h + j, hs) * EXPERTS + lax.rem(outer + d, EXPERTS)

    def slot_from(j, d):
        return lax.rem(h + hs - j, hs) * EXPERTS + lax.rem(outer + EXPERTS - d, EXPERTS)

    partner = at(outer, h, other)
    mine = h * EXPERTS + outer
    chips = [(j, d) for j in range(hs) for d in range(EXPERTS)]
    barrier = pltpu.get_barrier_semaphore()
    for j, d in chips:
        for c in (core, other):
            if (j, d) != (0, 0) or c is other:
                pl.semaphore_signal(barrier, inc=1, device_id=there(j, d, c), device_id_type=MESH)

    length = k_ref.shape[0] // 2
    cols = HALF * HEAD

    def half(c):
        return pl.ds(pl.multiple_of(c * cols, cols), cols)

    sources = [
        (q_hbm, q_ref),
        (dq_hbm, dq_ref),
        (gain_hbm, gain_ref),
        (dk_hbm.at[0], dk_ref),
        (dv_hbm.at[0], dv_ref),
        (k_hbm.at[:, half(core)], k_ref.at[pl.ds(0, length)]),
        (v_hbm.at[:, half(core)], v_ref.at[pl.ds(0, length)]),
        (wg_hbm.at[0], wg_ref),
        (wu_hbm.at[0], wu_ref),
        (wd_hbm.at[0], wd_ref),
        (len_hbm, len_ref),
        (idx_hbm, idx_ref),
        (gate_hbm, gate_ref),
    ]
    loads = [pltpu.make_async_copy(s, t, local.at[i]) for i, (s, t) in enumerate(sources)]
    for load in loads[:3] + loads[10:] + loads[3:7]:
        load.start()

    def remote(src, dst, ssem, rsem, peer):
        return pltpu.make_async_remote_copy(
            src_ref=src, dst_ref=dst, send_sem=ssem, recv_sem=rsem,
            device_id=peer, device_id_type=MESH,
        )

    tokens = q_ref.shape[0]
    rows = tokens + 1
    mt = MEM * tokens
    bs = MEM * CAP
    lanes = [slice(c * HEAD, (c + 1) * HEAD) for c in range(KV)]

    loads[0].wait()
    wide = q_ref[...].astype(F32)
    for c in range(KV):
        for m in range(MEM):
            i = c * MEM + m
            qs[c, m * tokens : (m + 1) * tokens, :] = wide[:, i * HEAD : (i + 1) * HEAD]
    for c in range(2):
        qh[c] = qs[c * HALF : (c + 1) * HALF].astype(BF)

    pl.semaphore_wait(barrier, n - 1)
    early = [
        remote(k_hbm.at[:, half(other)], k_ref.at[pl.ds(length, length)], psend.at[0], precv.at[0], partner),
        remote(v_hbm.at[:, half(other)], v_ref.at[pl.ds(length, length)], psend.at[1], precv.at[1], partner),
    ]
    qrows = 2 * mt

    def qslot(slot, count=1):
        return pl.ds(pl.multiple_of(slot * qrows, qrows), count * qrows)

    here = pl.ds(pl.multiple_of(mine * qrows + core * mt, mt), mt)
    sent = {}
    for j, d in chips:
        for rc in range(2):
            to = core if rc == 0 else other
            i = (j * EXPERTS + d) * 2 + rc
            if i:
                copy = remote(
                    qh.at[to], qg.at[:, here], qsend.at[i], qrecv.at[i], there(j, d, to)
                )
                copy.start()
                sent[i] = copy
    qg[:, here, :] = qh[core]
    for copy in early:
        copy.start()
    for load in loads[7:10]:
        load.start()
    for load in loads[10:]:
        load.wait()

    spots = []
    for r in range(rows):
        for t in range(idx_ref.shape[0]):
            named = idx_ref[t, r]
            spot = jnp.int32(0)
            for before in range(r):
                hit = (idx_ref[0, before] == named) | (idx_ref[1, before] == named)
                spot = spot + jnp.where(hit, 1, 0)
            spots.append((r, named, spot, gate_ref[t, r]))

    def token_of(i):
        return jnp.where(i < mt, lax.rem(i, tokens), jnp.where(i < mt + MEM, tokens, rows))

    def member_of(i):
        return jnp.where(i < mt, i // tokens, i - mt)

    side = xl.shape[0]
    a = lax.broadcasted_iota(jnp.int32, (EXPERTS * bs, side), 0)
    b = lax.broadcasted_iota(jnp.int32, (EXPERTS * bs, side), 1)
    same = lax.rem(a, bs) // CAP == member_of(b)
    pick = jnp.zeros((EXPERTS * bs, side), F32)
    code = a // bs * CAP + lax.rem(a, CAP)
    tok = jnp.where(same, token_of(b), rows)
    for r, named, spot, _ in spots:
        pick = jnp.where((tok == r) & (code == named * CAP + spot), 1.0, pick)
    pm[...] = pick.astype(BF)
    a = lax.broadcasted_iota(jnp.int32, (side, nc * bs), 0)
    b = lax.broadcasted_iota(jnp.int32, (side, nc * bs), 1)
    same = lax.rem(b, bs) // CAP == member_of(a)
    tok = jnp.where(same, token_of(a), rows)
    expert = lax.rem(outer + EXPERTS - lax.rem(b // bs, EXPERTS), EXPERTS)
    code = expert * CAP + lax.rem(b, CAP)
    mix = jnp.zeros((side, nc * bs), F32)
    for r, named, spot, gate in spots:
        mix = jnp.where((tok == r) & (code == named * CAP + spot), gate, mix)
    high = mix.astype(BF)
    gm[0] = high
    gm[1] = (mix - high.astype(F32)).astype(BF)

    scale = HEAD ** (-0.5)
    xl[...] = jnp.zeros(xl.shape, F32)
    iv[...] = jnp.zeros(iv.shape, F32)
    gs[...] = jnp.zeros(gs.shape, F32)
    loads[1].wait()
    loads[2].wait()
    wide = dq_ref[...].astype(F32)
    for c in range(KV):
        for m in range(MEM):
            i = c * MEM + m
            gain = gain_ref[:, i * HEAD : (i + 1) * HEAD]
            dqs[i : i + 1, :] = wide[:, i * HEAD : (i + 1) * HEAD]
            gs[m * tokens : (m + 1) * tokens, lanes[c]] = jnp.broadcast_to(gain, (tokens, HEAD))
            gs[mt + m : mt + m + 1, lanes[c]] = gain
    dq = dqs[...].astype(BF)
    dlen = dk_ref.shape[0]
    loads[3].wait()
    head_of = lax.broadcasted_iota(jnp.int32, (HEADS, dlen), 0) // MEM
    scores = jnp.zeros((HEADS, dlen), F32)
    for c in range(KV):
        part = lax.dot_general(
            dq, dk_ref[:, lanes[c]], (((1,), (1,)), ((), ())), preferred_element_type=F32
        )
        scores = jnp.where(head_of == c, part, scores)
    scores = scores * scale
    live = lax.broadcasted_iota(jnp.int32, (HEADS, dlen), 1) < len_ref[0]
    scores = jnp.where(live, scores, -1e30)
    peak = jnp.max(scores, axis=-1, keepdims=True)
    weights = jnp.where(live, jnp.exp(scores - peak), 0.0)
    total = jnp.sum(weights, axis=-1, keepdims=True)
    loads[4].wait()
    acc = jnp.zeros((HEADS, HEAD), F32)
    for c in range(KV):
        masked = jnp.where(head_of == c, weights, 0.0).astype(BF)
        acc = acc + jnp.dot(masked, dv_ref[:, lanes[c]], preferred_element_type=F32)
    dqs[...] = (acc / total).astype(BF).astype(F32)
    for c in range(KV):
        xl[mt : mt + MEM, lanes[c]] = dqs[c * MEM : (c + 1) * MEM, :]

    loads[5].wait()
    loads[6].wait()
    for copy in early:
        copy.wait_recv()
    returns = []
    count = EXPERTS * qrows
    a = lax.broadcasted_iota(jnp.int32, (HEAD, 2 * HEAD), 0)
    b = lax.broadcasted_iota(jnp.int32, (HEAD, 2 * HEAD), 1)
    spread = jnp.where(a == b // mt, 1.0, 0.0).astype(BF)
    a = lax.broadcasted_iota(jnp.int32, (count, 2 * HEAD), 0)
    b = lax.broadcasted_iota(jnp.int32, (count, 2 * HEAD), 1)
    sel = lax.rem(a, mt) == lax.rem(b, mt)
    lane = lax.broadcasted_iota(jnp.int32, (count, HEAD), 1)
    for j in range(hs):
        for i in range(j * EXPERTS * 2, (j + 1) * EXPERTS * 2):
            if i:
                sent[i].wait_recv()
        group = lax.rem(h + hs - j, hs)
        stats = jnp.zeros((count, HEAD), F32)
        first = pl.multiple_of(group * EXPERTS * 2, EXPERTS * 2)
        for c in range(HALF):
            sc = lax.dot_general(
                qg[c, qslot(group * EXPERTS, EXPERTS), :], k_ref[:, lanes[c]],
                (((1,), (1,)), ((), ())), preferred_element_type=F32,
            ) * scale
            pk = jnp.max(sc, axis=-1, keepdims=True).astype(BF).astype(F32)
            w = jnp.exp(sc - pk)
            tot = jnp.sum(w, axis=-1, keepdims=True)
            num = jnp.dot(w.astype(BF), v_ref[:, lanes[c]], preferred_element_type=F32)
            sb[pl.ds(first, EXPERTS * 2), c] = num.astype(BF).reshape(EXPERTS * 2, mt, HEAD)
            tot_high = tot.astype(BF).astype(F32)
            stats = jnp.where(lane == c, pk, stats)
            stats = jnp.where(lane == HALF + c, tot_high, stats)
            stats = jnp.where(lane == 2 * HALF + c, tot - tot_high, stats)
        compact = jnp.where(
            sel, jnp.dot(stats.astype(BF), spread, preferred_element_type=F32), 0.0
        )
        compact = jnp.sum(compact.reshape(EXPERTS * 2, mt, 2 * HEAD), axis=1)
        for i in range(EXPERTS * 2):
            st[first + i] = compact[i : i + 1]
        jj = (hs - j) % hs
        for d in sorted(range(EXPERTS), key=lambda d: -min(d, EXPERTS - d)):
            for rc in range(2):
                to = core if rc == 0 else other
                slot = slot_to(jj, d) * 2 + to
                i = (jj * EXPERTS + d) * 2 + rc
                pair = []
                for src, dst, ssem, rsem in (
                    (st.at[slot], rt.at[i], tsend.at[i], trecv.at[i]),
                    (sb.at[slot], rb.at[i], rsend.at[i], rrecv.at[i]),
                ):
                    if i == 0:
                        copy = pltpu.make_async_copy(src, dst, rsem)
                    else:
                        copy = remote(src, dst, ssem, rsem, there(jj, d, to))
                    copy.start()
                    pair.append(copy)
                returns.append((i, pair))
    returns.sort(key=lambda e: e[0])

    tr[...] = jnp.zeros(tr.shape, F32)
    low = lax.broadcasted_iota(jnp.int32, (nc, HEAD), 1) < HALF * mt
    scales = []
    for rc in range(2):
        found = list(range(rc, 2 * nc, 2))
        for i in found:
            copy = returns[i][1][0]
            copy.wait_recv() if i else copy.wait()
        stat = jnp.concatenate([rt[i] for i in found], axis=0)
        pk = stat[:, :HEAD]
        tot = pltpu.roll(pk, HALF * mt, 1) + stat[:, HEAD:]
        f = jnp.exp(jnp.minimum(pk - jnp.max(pk, axis=0, keepdims=True), 0.0))
        den = jnp.sum(jnp.where(low, f * tot, 1.0), axis=0, keepdims=True)
        tr[0:nc, :] = f / den
        scales.append(jnp.transpose(tr[...]))
    for rc in range(2):
        found = list(range(rc, 2 * nc, 2))
        source = core if rc == 0 else other
        for i in found:
            copy = returns[i][1][1]
            copy.wait_recv() if i else copy.wait()
        for c in range(HALF):
            acc = jnp.zeros((mt, HEAD), F32)
            for k, i in enumerate(found):
                acc = acc + rb[i, c].astype(F32) * scales[rc][c * mt : (c + 1) * mt, k : k + 1]
            xl[0:mt, pl.ds(pl.multiple_of(source * cols + c * HEAD, HEAD), HEAD)] = acc.astype(
                BF
            ).astype(F32)

    layer = xl[...]
    ss[...] = jnp.broadcast_to(
        jnp.sum(layer * layer, axis=1, keepdims=True) / (HEADS * HEAD), ss.shape
    )
    pre = ss[0:tokens, :]
    dec = ss[mt : mt + 1, :]
    for m in range(1, MEM):
        pre = pre + ss[m * tokens : (m + 1) * tokens, :]
        dec = dec + ss[mt + m : mt + m + 1, :]
    pre = lax.rsqrt(pre + 1e-05)
    for m in range(MEM):
        iv[m * tokens : (m + 1) * tokens, :] = pre
    iv[mt : mt + MEM, :] = jnp.broadcast_to(lax.rsqrt(dec + 1e-05), (MEM, HEAD))
    inv = iv[...]
    def xrow(slot, c):
        return pl.ds(pl.multiple_of((c * nc + slot) * bs, bs), bs)

    per = KV // PARTS
    moved = []
    for p in range(PARTS):
        block = lanes[p * per : (p + 1) * per]
        normed = jnp.concatenate([layer[:, s] * inv * gs[:, s] for s in block], axis=1).astype(BF)
        xs[p] = (
            jnp.dot(pm[...], normed, preferred_element_type=F32)
            .astype(BF)
            .reshape(EXPERTS, bs, per * HEAD)
        )
        out = {}
        for j, d in sorted(chips[1:], key=lambda jd: -(min(jd[1], EXPERTS - jd[1]) + (jd[0] > 0))):
            i = j * EXPERTS + d
            copy = remote(
                xs.at[p, lax.rem(outer + d, EXPERTS)], xg.at[p, xrow(mine, core)],
                gsend.at[p, i], grecv.at[p, i], there(j, d, core),
            )
            copy.start()
            out[j, d] = copy
        moved.append(out)
    shared = [[] for _ in range(PARTS)]
    arrival = sorted(chips[1:], key=lambda jd: (min(jd[1], EXPERTS - jd[1]) + (jd[0] > 0)))

    def widen(p, where):
        for c in range(per):
            xf[p * per + c, where, :] = xg[p, where, lanes[c]].astype(F32)

    def first_half(p):
        where = xrow(mine, core)
        i = 2 + p * nc
        copy = remote(
            xs.at[p, outer], xg.at[p, where], psend.at[i], precv.at[i], partner
        )
        copy.start()
        shared[p].append(copy)
        xg[p, where, :] = xs[p, outer]
        widen(p, where)
        for j, d in arrival:
            moved[p][j, d].wait_recv()
            where = xrow(slot_from(j, d), core)
            i = 2 + p * nc + j * EXPERTS + d
            copy = remote(xg.at[p, where], xg.at[p, where], psend.at[i], precv.at[i], partner)
            copy.start()
            shared[p].append(copy)
            widen(p, where)

    def second_half(p):
        for copy, (j, d) in zip(shared[p], [(0, 0)] + arrival):
            copy.wait_recv()
            widen(p, xrow(slot_from(j, d), other))
        for k in range(CAP):
            for c in range(p * per, (p + 1) * per):
                for m in range(MEM):
                    i = c * MEM + m
                    x[k * n : (k + 1) * n, i * HEAD : (i + 1) * HEAD] = xf[
                        c, pl.ds(m * CAP + k, n, stride=bs), :
                    ].astype(BF)

    ff = wg_ref.shape[1]
    step = 256 if ff % 256 == 0 else ff
    steps = ff // step
    deep = per * MEM * HEAD

    def up(p, i, carry):
        where = pl.ds(pl.multiple_of(i * step, step), step) if step != ff else slice(None)
        part = slice(p * deep, (p + 1) * deep)
        gated = jnp.dot(x[:, part], wg_ref[part, where], preferred_element_type=F32)
        raised = jnp.dot(x[:, part], wu_ref[part, where], preferred_element_type=F32)
        if p:
            gated = gated + ga[:, where]
            raised = raised + ua[:, where]
        if p < PARTS - 1:
            ga[:, where] = gated
            ua[:, where] = raised
        else:
            hid[:, where] = (gated / (1.0 + jnp.exp(-gated)) * raised).astype(BF)
        return carry

    first_half(0)
    second_half(0)
    for load in loads[7:9]:
        load.wait()
    for p in range(PARTS):
        middle = (steps * 4) // 7 if p < PARTS - 1 else steps
        lax.fori_loop(0, middle, functools.partial(up, p), 0)
        if p < PARTS - 1:
            first_half(p + 1)
            lax.fori_loop(middle, steps, functools.partial(up, p), 0)
            second_half(p + 1)
    loads[9].wait()

    each = KV // CHUNKS
    width = each * HEAD
    far = nc * bs
    swaps = []
    for g in range(CHUNKS):
        for e in range(each):
            c = g * each + e
            piece = jnp.dot(
                hid[...], wd_ref[:, c * MEM * HEAD : (c + 1) * MEM * HEAD], preferred_element_type=F32
            ).astype(BF).astype(F32)
            for k in range(CAP):
                for m in range(MEM):
                    pf[c, pl.ds(m * CAP + k, n, stride=bs), :] = piece[k * n : (k + 1) * n, lanes[m]]
            pb[g, :, lanes[e]] = pf[c, pl.ds(pl.multiple_of(other * far, far), far), :].astype(BF)
        i = 2 + PARTS * nc + g
        copy = remote(pb.at[g], p1.at[g], psend.at[i], precv.at[i], partner)
        copy.start()
        swaps.append(copy)
    outs = []
    for g in range(CHUNKS):
        swaps[g].wait_recv()
        for e in range(each):
            c = g * each + e
            ys[g, :, lanes[e]] = (
                pf[c, pl.ds(pl.multiple_of(core * far, far), far), :]
                + p1[g, :, lanes[e]].astype(F32)
            ).astype(BF)
        for o in range(EXPERTS):
            for hh in range(hs):
                d = lax.rem(o + EXPERTS - outer, EXPERTS)
                j = lax.rem(hh + hs - h, hs)
                i = j * EXPERTS + d

                @pl.when(i != 0)
                def _(o=o, hh=hh, i=i, g=g):
                    remote(
                        ys.at[g, pl.ds((hh * EXPERTS + o) * bs, bs)],
                        yr.at[g, pl.ds(pl.multiple_of(i * bs, bs), bs)],
                        ysend.at[g, i], yrecv.at[g, i], at(o, hh, core),
                    ).start()

        for i in range(1, nc):
            outs.append(
                remote(
                    ys.at[g, pl.ds(i * bs, bs)], yr.at[g, pl.ds(i * bs, bs)],
                    ysend.at[g, i], yrecv.at[g, i], partner,
                )
            )
        yr[g, 0:bs, :] = ys[g, pl.ds(pl.multiple_of(mine * bs, bs), bs), :]
    each_out = nc - 1
    for g in range(CHUNKS):
        for copy in outs[g * each_out : (g + 1) * each_out]:
            copy.wait_recv()
        where = slice(g * width, (g + 1) * width)
        osc[:, where] = (
            xl[:, where]
            + jnp.dot(gm[0], yr[g], preferred_element_type=F32)
            + jnp.dot(gm[1], yr[g], preferred_element_type=F32)
        )
    for c in range(KV):
        for m in range(MEM):
            i = c * MEM + m
            out_ref[0:tokens, i * HEAD : (i + 1) * HEAD] = osc[
                m * tokens : (m + 1) * tokens, lanes[c]
            ].astype(BF)
            out_ref[tokens:rows, i * HEAD : (i + 1) * HEAD] = osc[
                mt + m : mt + m + 1, lanes[c]
            ].astype(BF)
    for copy in early + list(sent.values()) + swaps + outs:
        copy.wait_send()
    for p in range(PARTS):
        for copy in list(moved[p].values()) + shared[p]:
            copy.wait_send()
    for i, pair in returns:
        if i:
            for copy in pair:
                copy.wait_send()


def on_device(n, *args):
    (q, k, v, dq, dk, dv, dlen, idx, gate, gain, wg, wu, wd) = args
    width = q.shape[1]
    tokens = q.shape[0]
    rows = tokens + dq.shape[0]
    nc = n // 2
    ff = wg.shape[2]
    mt, bs = MEM * tokens, MEM * CAP
    side = (mt + MEM + 15) // 16 * 16
    lanes = KV * HEAD
    hbm = pl.BlockSpec(memory_space=pl.ANY)
    vm = pl.BlockSpec(memory_space=pltpu.VMEM)
    positions = 2 * k.shape[0]
    dma = pltpu.SemaphoreType.DMA
    out = pl.pallas_call(
        functools.partial(body, n),
        out_shape=jax.ShapeDtypeStruct((rows, width), BF),
        in_specs=[hbm] * 13,
        out_specs=vm,
        scratch_shapes=[
            pltpu.SMEM(dlen.shape, jnp.int32),
            pltpu.SMEM(idx.T.shape, jnp.int32),
            pltpu.SMEM(gate.T.shape, F32),
            pltpu.VMEM(q.shape, BF),
            pltpu.VMEM(dq.shape, BF),
            pltpu.VMEM((1, width), F32),
            pltpu.VMEM((positions, HALF * HEAD), BF),
            pltpu.VMEM((positions, HALF * HEAD), BF),
            pltpu.VMEM(dk.shape[1:], BF),
            pltpu.VMEM(dv.shape[1:], BF),
            pltpu.VMEM(wg.shape[1:], BF),
            pltpu.VMEM(wu.shape[1:], BF),
            pltpu.VMEM(wd.shape[1:], BF),
            pltpu.VMEM((KV, mt, HEAD), F32),
            pltpu.VMEM((2, HALF, mt, HEAD), BF),
            pltpu.VMEM((HALF, nc * 2 * mt, HEAD), BF),
            pltpu.VMEM((n, HALF, mt, HEAD), BF),
            pltpu.VMEM((n, HALF, mt, HEAD), BF),
            pltpu.VMEM((n, 1, 2 * HEAD), F32),
            pltpu.VMEM((n, 1, 2 * HEAD), F32),
            pltpu.VMEM((HEAD, HEAD), F32),
            pltpu.VMEM((HEADS, HEAD), F32),
            pltpu.VMEM((side, lanes), F32),
            pltpu.VMEM((side, lanes), F32),
            pltpu.VMEM((side, HEAD), F32),
            pltpu.VMEM((side, HEAD), F32),
            pltpu.VMEM((EXPERTS * bs, side), BF),
            pltpu.VMEM((2, side, nc * bs), BF),
            pltpu.VMEM((PARTS, EXPERTS, bs, lanes // PARTS), BF),
            pltpu.VMEM((PARTS, n * bs, lanes // PARTS), BF),
            pltpu.VMEM((KV, n * bs, HEAD), F32),
            pltpu.VMEM((n * CAP, width), BF),
            pltpu.VMEM((n * CAP, ff), F32),
            pltpu.VMEM((n * CAP, ff), F32),
            pltpu.VMEM((n * CAP, ff), BF),
            pltpu.VMEM((KV, n * bs, HEAD), F32),
            pltpu.VMEM((CHUNKS, nc * bs, lanes // CHUNKS), BF),
            pltpu.VMEM((CHUNKS, nc * bs, lanes // CHUNKS), BF),
            pltpu.VMEM((CHUNKS, nc * bs, lanes // CHUNKS), BF),
            pltpu.VMEM((CHUNKS, nc * bs, lanes // CHUNKS), BF),
            pltpu.VMEM((side, lanes), F32),
            dma((n,)),
            dma((n,)),
            dma((PARTS, nc)),
            dma((PARTS, nc)),
            dma((n,)),
            dma((n,)),
            dma((n,)),
            dma((n,)),
            dma((2 + PARTS * nc + CHUNKS,)),
            dma((2 + PARTS * nc + CHUNKS,)),
            dma((CHUNKS, nc)),
            dma((CHUNKS, nc)),
            dma((13,)),
        ],
        compiler_params=pltpu.CompilerParams(
            collective_id=0, has_side_effects=True, vmem_limit_bytes=60_000_000
        ),
        name="moe_layer",
    )(q, dq, dlen, idx.T, gate.T, gain[None], k, v, dk, dv, wg, wu, wd)
    return out[:tokens], out[tokens:]


def solution(mesh):
    both = ("groups", "seq")
    in_specs = (
        P(both, None),
        P(both, None),
        P(both, None),
        P(both, None),
        P(both, None, None),
        P(both, None, None),
        P(both),
        P(both, None),
        P(both, None),
        P(),
        P("seq", None, None),
        P("seq", None, None),
        P("seq", None, None),
    )
    return jax.shard_map(
        functools.partial(on_device, mesh.shape["seq"]),
        mesh=mesh,
        in_specs=in_specs,
        out_specs=(P(both, None), P(both, None)),
        check_vma=False,
    )
```

```python
import functools

import jax
import jax.numpy as jnp
from jax import lax
from jax.experimental import pallas as pl
from jax.experimental.pallas import tpu as pltpu
from jax.sharding import PartitionSpec as P

HEADS = 32
KV = 8
MEM = HEADS // KV
HEAD = 128
EXPERTS = 4
CAP = 4
HALF = KV // 2
F32 = jnp.float32
BF = jnp.bfloat16
CHUNKS = 4
PARTS = 2
MESH = pl.DeviceIdType.MESH


def body(
    n,
    q_hbm,
    dq_hbm,
    len_hbm,
    idx_hbm,
    gate_hbm,
    gain_hbm,
    k_hbm,
    v_hbm,
    dk_hbm,
    dv_hbm,
    wg_hbm,
    wu_hbm,
    wd_hbm,
    out_ref,
    len_ref,
    idx_ref,
    gate_ref,
    q_ref,
    dq_ref,
    gain_ref,
    k_ref,
    v_ref,
    dk_ref,
    dv_ref,
    wg_ref,
    wu_ref,
    wd_ref,
    qs,
    qh,
    qg,
    sb,
    rb,
    st,
    rt,
    tr,
    dqs,
    gs,
    xl,
    ss,
    iv,
    pm,
    gm,
    xs,
    xg,
    xf,
    x,
    ga,
    ua,
    hid,
    pf,
    pb,
    p1,
    ys,
    yr,
    osc,
    qsend,
    qrecv,
    gsend,
    grecv,
    rsend,
    rrecv,
    tsend,
    trecv,
    psend,
    precv,
    ysend,
    yrecv,
    local,
):
    hs = n // (2 * EXPERTS)
    nc = hs * EXPERTS
    me = lax.axis_index("seq")
    core = lax.rem(me, 2)
    h = lax.rem(me // 2, hs)
    outer = me // (2 * hs)
    other = 1 - core

    def at(o, hh, c):
        return {"seq": (o * hs + hh) * 2 + c}

    def there(j, d, c):
        return at(lax.rem(outer + d, EXPERTS), lax.rem(h + j, hs), c)

    def slot_to(j, d):
        return lax.rem(h + j, hs) * EXPERTS + lax.rem(outer + d, EXPERTS)

    def slot_from(j, d):
        return lax.rem(h + hs - j, hs) * EXPERTS + lax.rem(outer + EXPERTS - d, EXPERTS)

    partner = at(outer, h, other)
    mine = h * EXPERTS + outer
    chips = [(j, d) for j in range(hs) for d in range(EXPERTS)]
    barrier = pltpu.get_barrier_semaphore()
    for j, d in chips:
        for c in (core, other):
            if (j, d) != (0, 0) or c is other:
                pl.semaphore_signal(barrier, inc=1, device_id=there(j, d, c), device_id_type=MESH)

    length = k_ref.shape[0] // 2
    cols = HALF * HEAD

    def half(c):
        return pl.ds(pl.multiple_of(c * cols, cols), cols)

    sources = [
        (q_hbm, q_ref),
        (dq_hbm, dq_ref),
        (gain_hbm, gain_ref),
        (dk_hbm.at[0], dk_ref),
        (dv_hbm.at[0], dv_ref),
        (k_hbm.at[:, half(core)], k_ref.at[pl.ds(0, length)]),
        (v_hbm.at[:, half(core)], v_ref.at[pl.ds(0, length)]),
        (wg_hbm.at[0], wg_ref),
        (wu_hbm.at[0], wu_ref),
        (wd_hbm.at[0], wd_ref),
        (len_hbm, len_ref),
        (idx_hbm, idx_ref),
        (gate_hbm, gate_ref),
    ]
    loads = [pltpu.make_async_copy(s, t, local.at[i]) for i, (s, t) in enumerate(sources)]
    for load in loads[:3] + loads[10:] + loads[3:7]:
        load.start()

    def remote(src, dst, ssem, rsem, peer):
        return pltpu.make_async_remote_copy(
            src_ref=src, dst_ref=dst, send_sem=ssem, recv_sem=rsem,
            device_id=peer, device_id_type=MESH,
        )

    tokens = q_ref.shape[0]
    rows = tokens + 1
    mt = MEM * tokens
    bs = MEM * CAP
    lanes = [slice(c * HEAD, (c + 1) * HEAD) for c in range(KV)]

    loads[0].wait()
    wide = q_ref[...].astype(F32)
    for c in range(KV):
        for m in range(MEM):
            i = c * MEM + m
            qs[c, m * tokens : (m + 1) * tokens, :] = wide[:, i * HEAD : (i + 1) * HEAD]
    for c in range(2):
        qh[c] = qs[c * HALF : (c + 1) * HALF].astype(BF)

    pl.semaphore_wait(barrier, n - 1)
    early = [
        remote(k_hbm.at[:, half(other)], k_ref.at[pl.ds(length, length)], psend.at[0], precv.at[0], partner),
        remote(v_hbm.at[:, half(other)], v_ref.at[pl.ds(length, length)], psend.at[1], precv.at[1], partner),
    ]
    qrows = 2 * mt

    def qslot(slot, count=1):
        return pl.ds(pl.multiple_of(slot * qrows, qrows), count * qrows)

    here = pl.ds(pl.multiple_of(mine * qrows + core * mt, mt), mt)
    sent = {}
    for j, d in chips:
        for rc in range(2):
            to = core if rc == 0 else other
            i = (j * EXPERTS + d) * 2 + rc
            if i:
                copy = remote(
                    qh.at[to], qg.at[:, here], qsend.at[i], qrecv.at[i], there(j, d, to)
                )
                copy.start()
                sent[i] = copy
    qg[:, here, :] = qh[core]
    for copy in early:
        copy.start()
    for load in loads[7:10]:
        load.start()
    for load in loads[10:]:
        load.wait()

    spots = []
    for r in range(rows):
        for t in range(idx_ref.shape[0]):
            named = idx_ref[t, r]
            spot = jnp.int32(0)
            for before in range(r):
                hit = (idx_ref[0, before] == named) | (idx_ref[1, before] == named)
                spot = spot + jnp.where(hit, 1, 0)
            spots.append((r, named, spot, gate_ref[t, r]))

    def token_of(i):
        return jnp.where(i < mt, lax.rem(i, tokens), jnp.where(i < mt + MEM, tokens, rows))

    def member_of(i):
        return jnp.where(i < mt, i // tokens, i - mt)

    side = xl.shape[0]
    a = lax.broadcasted_iota(jnp.int32, (EXPERTS * bs, side), 0)
    b = lax.broadcasted_iota(jnp.int32, (EXPERTS * bs, side), 1)
    same = lax.rem(a, bs) // CAP == member_of(b)
    pick = jnp.zeros((EXPERTS * bs, side), F32)
    code = a // bs * CAP + lax.rem(a, CAP)
    tok = jnp.where(same, token_of(b), rows)
    for r, named, spot, _ in spots:
        pick = jnp.where((tok == r) & (code == named * CAP + spot), 1.0, pick)
    pm[...] = pick.astype(BF)
    a = lax.broadcasted_iota(jnp.int32, (side, nc * bs), 0)
    b = lax.broadcasted_iota(jnp.int32, (side, nc * bs), 1)
    same = lax.rem(b, bs) // CAP == member_of(a)
    tok = jnp.where(same, token_of(a), rows)
    expert = lax.rem(outer + EXPERTS - lax.rem(b // bs, EXPERTS), EXPERTS)
    code = expert * CAP + lax.rem(b, CAP)
    mix = jnp.zeros((side, nc * bs), F32)
    for r, named, spot, gate in spots:
        mix = jnp.where((tok == r) & (code == named * CAP + spot), gate, mix)
    high = mix.astype(BF)
    gm[0] = high
    gm[1] = (mix - high.astype(F32)).astype(BF)

    scale = HEAD ** (-0.5)
    xl[...] = jnp.zeros(xl.shape, F32)
    iv[...] = jnp.zeros(iv.shape, F32)
    gs[...] = jnp.zeros(gs.shape, F32)
    loads[1].wait()
    loads[2].wait()
    wide = dq_ref[...].astype(F32)
    for c in range(KV):
        for m in range(MEM):
            i = c * MEM + m
            gain = gain_ref[:, i * HEAD : (i + 1) * HEAD]
            dqs[i : i + 1, :] = wide[:, i * HEAD : (i + 1) * HEAD]
            gs[m * tokens : (m + 1) * tokens, lanes[c]] = jnp.broadcast_to(gain, (tokens, HEAD))
            gs[mt + m : mt + m + 1, lanes[c]] = gain
    dq = dqs[...].astype(BF)
    dlen = dk_ref.shape[0]
    loads[3].wait()
    head_of = lax.broadcasted_iota(jnp.int32, (HEADS, dlen), 0) // MEM
    scores = jnp.zeros((HEADS, dlen), F32)
    for c in range(KV):
        part = lax.dot_general(
            dq, dk_ref[:, lanes[c]], (((1,), (1,)), ((), ())), preferred_element_type=F32
        )
        scores = jnp.where(head_of == c, part, scores)
    scores = scores * scale
    live = lax.broadcasted_iota(jnp.int32, (HEADS, dlen), 1) < len_ref[0]
    scores = jnp.where(live, scores, -1e30)
    peak = jnp.max(scores, axis=-1, keepdims=True)
    weights = jnp.where(live, jnp.exp(scores - peak), 0.0)
    total = jnp.sum(weights, axis=-1, keepdims=True)
    loads[4].wait()
    acc = jnp.zeros((HEADS, HEAD), F32)
    for c in range(KV):
        masked = jnp.where(head_of == c, weights, 0.0).astype(BF)
        acc = acc + jnp.dot(masked, dv_ref[:, lanes[c]], preferred_element_type=F32)
    dqs[...] = (acc / total).astype(BF).astype(F32)
    for c in range(KV):
        xl[mt : mt + MEM, lanes[c]] = dqs[c * MEM : (c + 1) * MEM, :]

    loads[5].wait()
    loads[6].wait()
    for copy in early:
        copy.wait_recv()
    returns = []
    count = EXPERTS * qrows
    a = lax.broadcasted_iota(jnp.int32, (HEAD, 2 * HEAD), 0)
    b = lax.broadcasted_iota(jnp.int32, (HEAD, 2 * HEAD), 1)
    spread = jnp.where(a == b // mt, 1.0, 0.0).astype(BF)
    a = lax.broadcasted_iota(jnp.int32, (count, 2 * HEAD), 0)
    b = lax.broadcasted_iota(jnp.int32, (count, 2 * HEAD), 1)
    sel = lax.rem(a, mt) == lax.rem(b, mt)
    lane = lax.broadcasted_iota(jnp.int32, (count, HEAD), 1)
    for j in range(hs):
        for i in range(j * EXPERTS * 2, (j + 1) * EXPERTS * 2):
            if i:
                sent[i].wait_recv()
        group = lax.rem(h + hs - j, hs)
        stats = jnp.zeros((count, HEAD), F32)
        first = pl.multiple_of(group * EXPERTS * 2, EXPERTS * 2)
        for c in range(HALF):
            sc = lax.dot_general(
                qg[c, qslot(group * EXPERTS, EXPERTS), :], k_ref[:, lanes[c]],
                (((1,), (1,)), ((), ())), preferred_element_type=F32,
            ) * scale
            pk = jnp.max(sc, axis=-1, keepdims=True).astype(BF).astype(F32)
            w = jnp.exp(sc - pk)
            tot = jnp.sum(w, axis=-1, keepdims=True)
            num = jnp.dot(w.astype(BF), v_ref[:, lanes[c]], preferred_element_type=F32)
            sb[pl.ds(first, EXPERTS * 2), c] = num.astype(BF).reshape(EXPERTS * 2, mt, HEAD)
            tot_high = tot.astype(BF).astype(F32)
            stats = jnp.where(lane == c, pk, stats)
            stats = jnp.where(lane == HALF + c, tot_high, stats)
            stats = jnp.where(lane == 2 * HALF + c, tot - tot_high, stats)
        compact = jnp.where(
            sel, jnp.dot(stats.astype(BF), spread, preferred_element_type=F32), 0.0
        )
        compact = jnp.sum(compact.reshape(EXPERTS * 2, mt, 2 * HEAD), axis=1)
        for i in range(EXPERTS * 2):
            st[first + i] = compact[i : i + 1]
        jj = (hs - j) % hs
        for d in sorted(range(EXPERTS), key=lambda d: -min(d, EXPERTS - d)):
            for rc in range(2):
                to = core if rc == 0 else other
                slot = slot_to(jj, d) * 2 + to
                i = (jj * EXPERTS + d) * 2 + rc
                pair = []
                for src, dst, ssem, rsem in (
                    (st.at[slot], rt.at[i], tsend.at[i], trecv.at[i]),
                    (sb.at[slot], rb.at[i], rsend.at[i], rrecv.at[i]),
                ):
                    if i == 0:
                        copy = pltpu.make_async_copy(src, dst, rsem)
                    else:
                        copy = remote(src, dst, ssem, rsem, there(jj, d, to))
                    copy.start()
                    pair.append(copy)
                returns.append((i, pair))
    returns.sort(key=lambda e: e[0])

    tr[...] = jnp.zeros(tr.shape, F32)
    low = lax.broadcasted_iota(jnp.int32, (nc, HEAD), 1) < HALF * mt
    scales = []
    for rc in range(2):
        found = list(range(rc, 2 * nc, 2))
        for i in found:
            copy = returns[i][1][0]
            copy.wait_recv() if i else copy.wait()
        stat = jnp.concatenate([rt[i] for i in found], axis=0)
        pk = stat[:, :HEAD]
        tot = pltpu.roll(pk, HALF * mt, 1) + stat[:, HEAD:]
        f = jnp.exp(jnp.minimum(pk - jnp.max(pk, axis=0, keepdims=True), 0.0))
        den = jnp.sum(jnp.where(low, f * tot, 1.0), axis=0, keepdims=True)
        tr[0:nc, :] = f / den
        scales.append(jnp.transpose(tr[...]))
    for rc in range(2):
        found = list(range(rc, 2 * nc, 2))
        source = core if rc == 0 else other
        for i in found:
            copy = returns[i][1][1]
            copy.wait_recv() if i else copy.wait()
        for c in range(HALF):
            acc = jnp.zeros((mt, HEAD), F32)
            for k, i in enumerate(found):
                acc = acc + rb[i, c].astype(F32) * scales[rc][c * mt : (c + 1) * mt, k : k + 1]
            xl[0:mt, pl.ds(pl.multiple_of(source * cols + c * HEAD, HEAD), HEAD)] = acc.astype(
                BF
            ).astype(F32)

    layer = xl[...]
    ss[...] = jnp.broadcast_to(
        jnp.sum(layer * layer, axis=1, keepdims=True) / (HEADS * HEAD), ss.shape
    )
    pre = ss[0:tokens, :]
    dec = ss[mt : mt + 1, :]
    for m in range(1, MEM):
        pre = pre + ss[m * tokens : (m + 1) * tokens, :]
        dec = dec + ss[mt + m : mt + m + 1, :]
    pre = lax.rsqrt(pre + 1e-05)
    for m in range(MEM):
        iv[m * tokens : (m + 1) * tokens, :] = pre
    iv[mt : mt + MEM, :] = jnp.broadcast_to(lax.rsqrt(dec + 1e-05), (MEM, HEAD))
    inv = iv[...]
    def xrow(slot, c):
        return pl.ds(pl.multiple_of((c * nc + slot) * bs, bs), bs)

    per = KV // PARTS
    moved = []
    for p in range(PARTS):
        block = lanes[p * per : (p + 1) * per]
        normed = jnp.concatenate([layer[:, s] * inv * gs[:, s] for s in block], axis=1).astype(BF)
        xs[p] = (
            jnp.dot(pm[...], normed, preferred_element_type=F32)
            .astype(BF)
            .reshape(EXPERTS, bs, per * HEAD)
        )
        out = {}
        for j, d in sorted(chips[1:], key=lambda jd: -(min(jd[1], EXPERTS - jd[1]) + (jd[0] > 0))):
            i = j * EXPERTS + d
            copy = remote(
                xs.at[p, lax.rem(outer + d, EXPERTS)], xg.at[p, xrow(mine, core)],
                gsend.at[p, i], grecv.at[p, i], there(j, d, core),
            )
            copy.start()
            out[j, d] = copy
        moved.append(out)
    shared = [[] for _ in range(PARTS)]
    arrival = sorted(chips[1:], key=lambda jd: (min(jd[1], EXPERTS - jd[1]) + (jd[0] > 0)))

    def widen(p, where):
        for c in range(per):
            xf[p * per + c, where, :] = xg[p, where, lanes[c]].astype(F32)

    def first_half(p):
        where = xrow(mine, core)
        i = 2 + p * nc
        copy = remote(
            xs.at[p, outer], xg.at[p, where], psend.at[i], precv.at[i], partner
        )
        copy.start()
        shared[p].append(copy)
        xg[p, where, :] = xs[p, outer]
        widen(p, where)
        for j, d in arrival:
            moved[p][j, d].wait_recv()
            where = xrow(slot_from(j, d), core)
            i = 2 + p * nc + j * EXPERTS + d
            copy = remote(xg.at[p, where], xg.at[p, where], psend.at[i], precv.at[i], partner)
            copy.start()
            shared[p].append(copy)
            widen(p, where)

    def second_half(p):
        for copy, (j, d) in zip(shared[p], [(0, 0)] + arrival):
            copy.wait_recv()
            widen(p, xrow(slot_from(j, d), other))
        for k in range(CAP):
            for c in range(p * per, (p + 1) * per):
                for m in range(MEM):
                    i = c * MEM + m
                    x[k * n : (k + 1) * n, i * HEAD : (i + 1) * HEAD] = xf[
                        c, pl.ds(m * CAP + k, n, stride=bs), :
                    ].astype(BF)

    ff = wg_ref.shape[1]
    step = 256 if ff % 256 == 0 else ff
    steps = ff // step
    deep = per * MEM * HEAD

    def up(p, i, carry):
        where = pl.ds(pl.multiple_of(i * step, step), step) if step != ff else slice(None)
        part = slice(p * deep, (p + 1) * deep)
        gated = jnp.dot(x[:, part], wg_ref[part, where], preferred_element_type=F32)
        raised = jnp.dot(x[:, part], wu_ref[part, where], preferred_element_type=F32)
        if p:
            gated = gated + ga[:, where]
            raised = raised + ua[:, where]
        if p < PARTS - 1:
            ga[:, where] = gated
            ua[:, where] = raised
        else:
            hid[:, where] = (gated / (1.0 + jnp.exp(-gated)) * raised).astype(BF)
        return carry

    first_half(0)
    second_half(0)
    for load in loads[7:9]:
        load.wait()
    for p in range(PARTS):
        middle = (steps * 4) // 7 if p < PARTS - 1 else steps
        lax.fori_loop(0, middle, functools.partial(up, p), 0)
        if p < PARTS - 1:
            first_half(p + 1)
            lax.fori_loop(middle, steps, functools.partial(up, p), 0)
            second_half(p + 1)
    loads[9].wait()

    each = KV // CHUNKS
    width = each * HEAD
    far = nc * bs
    swaps = []
    outs = []

    def down(g):
        for e in range(each):
            c = g * each + e
            piece = jnp.dot(
                hid[...], wd_ref[:, c * MEM * HEAD : (c + 1) * MEM * HEAD], preferred_element_type=F32
            ).astype(BF).astype(F32)
            for k in range(CAP):
                for m in range(MEM):
                    pf[c, pl.ds(m * CAP + k, n, stride=bs), :] = piece[k * n : (k + 1) * n, lanes[m]]
            pb[g, :, lanes[e]] = pf[c, pl.ds(pl.multiple_of(other * far, far), far), :].astype(BF)
        i = 2 + PARTS * nc + g
        copy = remote(pb.at[g], p1.at[g], psend.at[i], precv.at[i], partner)
        copy.start()
        swaps.append(copy)

    def deliver(g):
        swaps[g].wait_recv()
        for e in range(each):
            c = g * each + e
            ys[g, :, lanes[e]] = (
                pf[c, pl.ds(pl.multiple_of(core * far, far), far), :]
                + p1[g, :, lanes[e]].astype(F32)
            ).astype(BF)
        for o in range(EXPERTS):
            for hh in range(hs):
                d = lax.rem(o + EXPERTS - outer, EXPERTS)
                j = lax.rem(hh + hs - h, hs)
                i = j * EXPERTS + d

                @pl.when(i != 0)
                def _(o=o, hh=hh, i=i, g=g):
                    remote(
                        ys.at[g, pl.ds((hh * EXPERTS + o) * bs, bs)],
                        yr.at[g, pl.ds(pl.multiple_of(i * bs, bs), bs)],
                        ysend.at[g, i], yrecv.at[g, i], at(o, hh, core),
                    ).start()

        for i in range(1, nc):
            outs.append(
                remote(
                    ys.at[g, pl.ds(i * bs, bs)], yr.at[g, pl.ds(i * bs, bs)],
                    ysend.at[g, i], yrecv.at[g, i], partner,
                )
            )
        yr[g, 0:bs, :] = ys[g, pl.ds(pl.multiple_of(mine * bs, bs), bs), :]

    for g in range(CHUNKS):
        down(g)
        if g:
            deliver(g - 1)
    deliver(CHUNKS - 1)
    each_out = nc - 1
    for g in range(CHUNKS):
        for copy in outs[g * each_out : (g + 1) * each_out]:
            copy.wait_recv()
        where = slice(g * width, (g + 1) * width)
        osc[:, where] = (
            xl[:, where]
            + jnp.dot(gm[0], yr[g], preferred_element_type=F32)
            + jnp.dot(gm[1], yr[g], preferred_element_type=F32)
        )
    for c in range(KV):
        for m in range(MEM):
            i = c * MEM + m
            out_ref[0:tokens, i * HEAD : (i + 1) * HEAD] = osc[
                m * tokens : (m + 1) * tokens, lanes[c]
            ].astype(BF)
            out_ref[tokens:rows, i * HEAD : (i + 1) * HEAD] = osc[
                mt + m : mt + m + 1, lanes[c]
            ].astype(BF)
    for copy in early + list(sent.values()) + swaps + outs:
        copy.wait_send()
    for p in range(PARTS):
        for copy in list(moved[p].values()) + shared[p]:
            copy.wait_send()
    for i, pair in returns:
        if i:
            for copy in pair:
                copy.wait_send()


def on_device(n, *args):
    (q, k, v, dq, dk, dv, dlen, idx, gate, gain, wg, wu, wd) = args
    width = q.shape[1]
    tokens = q.shape[0]
    rows = tokens + dq.shape[0]
    nc = n // 2
    ff = wg.shape[2]
    mt, bs = MEM * tokens, MEM * CAP
    side = (mt + MEM + 15) // 16 * 16
    lanes = KV * HEAD
    hbm = pl.BlockSpec(memory_space=pl.ANY)
    vm = pl.BlockSpec(memory_space=pltpu.VMEM)
    positions = 2 * k.shape[0]
    dma = pltpu.SemaphoreType.DMA
    out = pl.pallas_call(
        functools.partial(body, n),
        out_shape=pltpu.VMEM((rows, width), BF),
        in_specs=[hbm] * 13,
        out_specs=vm,
        scratch_shapes=[
            pltpu.SMEM(dlen.shape, jnp.int32),
            pltpu.SMEM(idx.T.shape, jnp.int32),
            pltpu.SMEM(gate.T.shape, F32),
            pltpu.VMEM(q.shape, BF),
            pltpu.VMEM(dq.shape, BF),
            pltpu.VMEM((1, width), F32),
            pltpu.VMEM((positions, HALF * HEAD), BF),
            pltpu.VMEM((positions, HALF * HEAD), BF),
            pltpu.VMEM(dk.shape[1:], BF),
            pltpu.VMEM(dv.shape[1:], BF),
            pltpu.VMEM(wg.shape[1:], BF),
            pltpu.VMEM(wu.shape[1:], BF),
            pltpu.VMEM(wd.shape[1:], BF),
            pltpu.VMEM((KV, mt, HEAD), F32),
            pltpu.VMEM((2, HALF, mt, HEAD), BF),
            pltpu.VMEM((HALF, nc * 2 * mt, HEAD), BF),
            pltpu.VMEM((n, HALF, mt, HEAD), BF),
            pltpu.VMEM((n, HALF, mt, HEAD), BF),
            pltpu.VMEM((n, 1, 2 * HEAD), F32),
            pltpu.VMEM((n, 1, 2 * HEAD), F32),
            pltpu.VMEM((HEAD, HEAD), F32),
            pltpu.VMEM((HEADS, HEAD), F32),
            pltpu.VMEM((side, lanes), F32),
            pltpu.VMEM((side, lanes), F32),
            pltpu.VMEM((side, HEAD), F32),
            pltpu.VMEM((side, HEAD), F32),
            pltpu.VMEM((EXPERTS * bs, side), BF),
            pltpu.VMEM((2, side, nc * bs), BF),
            pltpu.VMEM((PARTS, EXPERTS, bs, lanes // PARTS), BF),
            pltpu.VMEM((PARTS, n * bs, lanes // PARTS), BF),
            pltpu.VMEM((KV, n * bs, HEAD), F32),
            pltpu.VMEM((n * CAP, width), BF),
            pltpu.VMEM((n * CAP, ff), F32),
            pltpu.VMEM((n * CAP, ff), F32),
            pltpu.VMEM((n * CAP, ff), BF),
            pltpu.VMEM((KV, n * bs, HEAD), F32),
            pltpu.VMEM((CHUNKS, nc * bs, lanes // CHUNKS), BF),
            pltpu.VMEM((CHUNKS, nc * bs, lanes // CHUNKS), BF),
            pltpu.VMEM((CHUNKS, nc * bs, lanes // CHUNKS), BF),
            pltpu.VMEM((CHUNKS, nc * bs, lanes // CHUNKS), BF),
            pltpu.VMEM((side, lanes), F32),
            dma((n,)),
            dma((n,)),
            dma((PARTS, nc)),
            dma((PARTS, nc)),
            dma((n,)),
            dma((n,)),
            dma((n,)),
            dma((n,)),
            dma((2 + PARTS * nc + CHUNKS,)),
            dma((2 + PARTS * nc + CHUNKS,)),
            dma((CHUNKS, nc)),
            dma((CHUNKS, nc)),
            dma((13,)),
        ],
        compiler_params=pltpu.CompilerParams(
            collective_id=0, has_side_effects=True, vmem_limit_bytes=60_000_000
        ),
        name="moe_layer",
    )(q, dq, dlen, idx.T, gate.T, gain[None], k, v, dk, dv, wg, wu, wd)
    return out[:tokens], out[tokens:]


def solution(mesh):
    both = ("groups", "seq")
    in_specs = (
        P(both, None),
        P(both, None),
        P(both, None),
        P(both, None),
        P(both, None, None),
        P(both, None, None),
        P(both),
        P(both, None),
        P(both, None),
        P(),
        P("seq", None, None),
        P("seq", None, None),
        P("seq", None, None),
    )
    return jax.shard_map(
        functools.partial(on_device, mesh.shape["seq"]),
        mesh=mesh,
        in_specs=in_specs,
        out_specs=(P(both, None), P(both, None)),
        check_vma=False,
    )
```

```python
import functools

import jax
import jax.numpy as jnp
from jax import lax
from jax.experimental import pallas as pl
from jax.experimental.pallas import tpu as pltpu
from jax.sharding import PartitionSpec as P

HEADS = 32
KV = 8
MEM = HEADS // KV
HEAD = 128
EXPERTS = 4
CAP = 4
HALF = KV // 2
F32 = jnp.float32
BF = jnp.bfloat16
CHUNKS = 4
FULL = 128
PARTS = 2
MESH = pl.DeviceIdType.MESH


def body(
    n,
    q_hbm,
    dq_hbm,
    len_hbm,
    idx_hbm,
    gate_hbm,
    gain_hbm,
    k_hbm,
    v_hbm,
    dk_hbm,
    dv_hbm,
    wg_hbm,
    wu_hbm,
    wd_hbm,
    out_ref,
    len_ref,
    idx_ref,
    gate_ref,
    q_ref,
    dq_ref,
    gain_ref,
    k_ref,
    v_ref,
    dk_ref,
    dv_ref,
    wg_ref,
    wu_ref,
    wd_ref,
    qs,
    qh,
    qg,
    sb,
    rb,
    st,
    rt,
    tr,
    dqs,
    gs,
    xl,
    ss,
    iv,
    pm,
    gm,
    xs,
    xg,
    xf,
    x,
    ga,
    ua,
    hid,
    pf,
    pb,
    p1,
    ys,
    yr,
    osc,
    qsend,
    qrecv,
    gsend,
    grecv,
    rsend,
    rrecv,
    tsend,
    trecv,
    psend,
    precv,
    ysend,
    yrecv,
    local,
):
    hs = n // (2 * EXPERTS)
    nc = hs * EXPERTS
    me = lax.axis_index("seq")
    core = lax.rem(me, 2)
    h = lax.rem(me // 2, hs)
    outer = me // (2 * hs)
    other = 1 - core

    def at(o, hh, c):
        return {"seq": (o * hs + hh) * 2 + c}

    def there(j, d, c):
        return at(lax.rem(outer + d, EXPERTS), lax.rem(h + j, hs), c)

    def slot_to(j, d):
        return lax.rem(h + j, hs) * EXPERTS + lax.rem(outer + d, EXPERTS)

    def slot_from(j, d):
        return lax.rem(h + hs - j, hs) * EXPERTS + lax.rem(outer + EXPERTS - d, EXPERTS)

    partner = at(outer, h, other)
    mine = h * EXPERTS + outer
    chips = [(j, d) for j in range(hs) for d in range(EXPERTS)]
    barrier = pltpu.get_barrier_semaphore()
    for j, d in chips:
        for c in (core, other):
            if (j, d) != (0, 0) or c is other:
                pl.semaphore_signal(barrier, inc=1, device_id=there(j, d, c), device_id_type=MESH)

    length = k_ref.shape[0] // 2
    cols = HALF * HEAD

    def half(c):
        return pl.ds(pl.multiple_of(c * cols, cols), cols)

    sources = [
        (q_hbm, q_ref),
        (dq_hbm, dq_ref),
        (gain_hbm, gain_ref),
        (dk_hbm.at[0], dk_ref),
        (dv_hbm.at[0], dv_ref),
        (k_hbm.at[:, half(core)], k_ref.at[pl.ds(0, length)]),
        (v_hbm.at[:, half(core)], v_ref.at[pl.ds(0, length)]),
        (wg_hbm.at[0], wg_ref),
        (wu_hbm.at[0], wu_ref),
        (wd_hbm.at[0], wd_ref),
        (len_hbm, len_ref),
        (idx_hbm, idx_ref),
        (gate_hbm, gate_ref),
    ]
    loads = [pltpu.make_async_copy(s, t, local.at[i]) for i, (s, t) in enumerate(sources)]
    for load in loads[:3] + loads[10:] + loads[3:7]:
        load.start()

    def remote(src, dst, ssem, rsem, peer):
        return pltpu.make_async_remote_copy(
            src_ref=src, dst_ref=dst, send_sem=ssem, recv_sem=rsem,
            device_id=peer, device_id_type=MESH,
        )

    tokens = q_ref.shape[0]
    rows = tokens + 1
    mt = MEM * tokens
    bs = MEM * CAP
    lanes = [slice(c * HEAD, (c + 1) * HEAD) for c in range(KV)]

    loads[0].wait()
    wide = q_ref[...].astype(F32)
    for c in range(KV):
        for m in range(MEM):
            i = c * MEM + m
            qs[c, m * tokens : (m + 1) * tokens, :] = wide[:, i * HEAD : (i + 1) * HEAD]
    for c in range(2):
        qh[c] = qs[c * HALF : (c + 1) * HALF].astype(BF)

    pl.semaphore_wait(barrier, n - 1)
    early = [
        remote(k_hbm.at[:, half(other)], k_ref.at[pl.ds(length, length)], psend.at[0], precv.at[0], partner),
        remote(v_hbm.at[:, half(other)], v_ref.at[pl.ds(length, length)], psend.at[1], precv.at[1], partner),
    ]
    qrows = 2 * mt

    def qslot(slot, count=1):
        return pl.ds(pl.multiple_of(slot * qrows, qrows), count * qrows)

    here = pl.ds(pl.multiple_of(mine * qrows + core * mt, mt), mt)
    sent = {}
    for j, d in chips:
        for rc in range(2):
            to = core if rc == 0 else other
            i = (j * EXPERTS + d) * 2 + rc
            if i:
                copy = remote(
                    qh.at[to], qg.at[:, here], qsend.at[i], qrecv.at[i], there(j, d, to)
                )
                copy.start()
                sent[i] = copy
    qg[:, here, :] = qh[core]
    for copy in early:
        copy.start()
    for load in loads[7:10]:
        load.start()
    for load in loads[10:]:
        load.wait()

    spots = []
    for r in range(rows):
        for t in range(idx_ref.shape[0]):
            named = idx_ref[t, r]
            spot = jnp.int32(0)
            for before in range(r):
                hit = (idx_ref[0, before] == named) | (idx_ref[1, before] == named)
                spot = spot + jnp.where(hit, 1, 0)
            spots.append((r, named, spot, gate_ref[t, r]))

    def token_of(i):
        return jnp.where(i < mt, lax.rem(i, tokens), jnp.where(i < mt + MEM, tokens, rows))

    def member_of(i):
        return jnp.where(i < mt, i // tokens, i - mt)

    side = xl.shape[0]
    a = lax.broadcasted_iota(jnp.int32, (EXPERTS * bs, side), 0)
    b = lax.broadcasted_iota(jnp.int32, (EXPERTS * bs, side), 1)
    same = lax.rem(a, bs) // CAP == member_of(b)
    pick = jnp.zeros((EXPERTS * bs, side), F32)
    code = a // bs * CAP + lax.rem(a, CAP)
    tok = jnp.where(same, token_of(b), rows)
    for r, named, spot, _ in spots:
        pick = jnp.where((tok == r) & (code == named * CAP + spot), 1.0, pick)
    pm[...] = pick.astype(BF)
    a = lax.broadcasted_iota(jnp.int32, (side, nc * bs), 0)
    b = lax.broadcasted_iota(jnp.int32, (side, nc * bs), 1)
    same = lax.rem(b, bs) // CAP == member_of(a)
    tok = jnp.where(same, token_of(a), rows)
    expert = lax.rem(outer + EXPERTS - lax.rem(b // bs, EXPERTS), EXPERTS)
    code = expert * CAP + lax.rem(b, CAP)
    mix = jnp.zeros((side, nc * bs), F32)
    for r, named, spot, gate in spots:
        mix = jnp.where((tok == r) & (code == named * CAP + spot), gate, mix)
    high = mix.astype(BF)
    gm[0] = high
    gm[1] = (mix - high.astype(F32)).astype(BF)

    scale = HEAD ** (-0.5)
    if x.shape[0] > n * CAP:
        x[n * CAP :, :] = jnp.zeros((x.shape[0] - n * CAP, x.shape[1]), BF)
    xl[...] = jnp.zeros(xl.shape, F32)
    iv[...] = jnp.zeros(iv.shape, F32)
    gs[...] = jnp.zeros(gs.shape, F32)
    loads[1].wait()
    loads[2].wait()
    wide = dq_ref[...].astype(F32)
    for c in range(KV):
        for m in range(MEM):
            i = c * MEM + m
            gain = gain_ref[:, i * HEAD : (i + 1) * HEAD]
            dqs[i : i + 1, :] = wide[:, i * HEAD : (i + 1) * HEAD]
            gs[m * tokens : (m + 1) * tokens, lanes[c]] = jnp.broadcast_to(gain, (tokens, HEAD))
            gs[mt + m : mt + m + 1, lanes[c]] = gain
    dq = dqs[...].astype(BF)
    dlen = dk_ref.shape[0]
    loads[3].wait()
    head_of = lax.broadcasted_iota(jnp.int32, (HEADS, dlen), 0) // MEM
    scores = jnp.zeros((HEADS, dlen), F32)
    for c in range(KV):
        part = lax.dot_general(
            dq, dk_ref[:, lanes[c]], (((1,), (1,)), ((), ())), preferred_element_type=F32
        )
        scores = jnp.where(head_of == c, part, scores)
    scores = scores * scale
    live = lax.broadcasted_iota(jnp.int32, (HEADS, dlen), 1) < len_ref[0]
    scores = jnp.where(live, scores, -1e30)
    peak = jnp.max(scores, axis=-1, keepdims=True)
    weights = jnp.where(live, jnp.exp(scores - peak), 0.0)
    total = jnp.sum(weights, axis=-1, keepdims=True)
    loads[4].wait()
    acc = jnp.zeros((HEADS, HEAD), F32)
    for c in range(KV):
        masked = jnp.where(head_of == c, weights, 0.0).astype(BF)
        acc = acc + jnp.dot(masked, dv_ref[:, lanes[c]], preferred_element_type=F32)
    dqs[...] = (acc / total).astype(BF).astype(F32)
    for c in range(KV):
        xl[mt : mt + MEM, lanes[c]] = dqs[c * MEM : (c + 1) * MEM, :]

    loads[5].wait()
    loads[6].wait()
    for copy in early:
        copy.wait_recv()
    returns = []
    count = EXPERTS * qrows
    a = lax.broadcasted_iota(jnp.int32, (HEAD, 2 * HEAD), 0)
    b = lax.broadcasted_iota(jnp.int32, (HEAD, 2 * HEAD), 1)
    spread = jnp.where(a == b // mt, 1.0, 0.0).astype(BF)
    a = lax.broadcasted_iota(jnp.int32, (count, 2 * HEAD), 0)
    b = lax.broadcasted_iota(jnp.int32, (count, 2 * HEAD), 1)
    sel = lax.rem(a, mt) == lax.rem(b, mt)
    lane = lax.broadcasted_iota(jnp.int32, (count, HEAD), 1)
    for j in range(hs):
        for i in range(j * EXPERTS * 2, (j + 1) * EXPERTS * 2):
            if i:
                sent[i].wait_recv()
        group = lax.rem(h + hs - j, hs)
        stats = jnp.zeros((count, HEAD), F32)
        first = pl.multiple_of(group * EXPERTS * 2, EXPERTS * 2)
        for c in range(HALF):
            sc = lax.dot_general(
                qg[c, qslot(group * EXPERTS, EXPERTS), :], k_ref[:, lanes[c]],
                (((1,), (1,)), ((), ())), preferred_element_type=F32,
            ) * scale
            pk = jnp.max(sc, axis=-1, keepdims=True).astype(BF).astype(F32)
            w = jnp.exp(sc - pk)
            tot = jnp.sum(w, axis=-1, keepdims=True)
            num = jnp.dot(w.astype(BF), v_ref[:, lanes[c]], preferred_element_type=F32)
            sb[pl.ds(first, EXPERTS * 2), c] = num.astype(BF).reshape(EXPERTS * 2, mt, HEAD)
            tot_high = tot.astype(BF).astype(F32)
            stats = jnp.where(lane == c, pk, stats)
            stats = jnp.where(lane == HALF + c, tot_high, stats)
            stats = jnp.where(lane == 2 * HALF + c, tot - tot_high, stats)
        compact = jnp.where(
            sel, jnp.dot(stats.astype(BF), spread, preferred_element_type=F32), 0.0
        )
        compact = jnp.sum(compact.reshape(EXPERTS * 2, mt, 2 * HEAD), axis=1)
        for i in range(EXPERTS * 2):
            st[first + i] = compact[i : i + 1]
        jj = (hs - j) % hs
        for d in sorted(range(EXPERTS), key=lambda d: -min(d, EXPERTS - d)):
            for rc in range(2):
                to = core if rc == 0 else other
                slot = slot_to(jj, d) * 2 + to
                i = (jj * EXPERTS + d) * 2 + rc
                pair = []
                for src, dst, ssem, rsem in (
                    (st.at[slot], rt.at[i], tsend.at[i], trecv.at[i]),
                    (sb.at[slot], rb.at[i], rsend.at[i], rrecv.at[i]),
                ):
                    if i == 0:
                        copy = pltpu.make_async_copy(src, dst, rsem)
                    else:
                        copy = remote(src, dst, ssem, rsem, there(jj, d, to))
                    copy.start()
                    pair.append(copy)
                returns.append((i, pair))
    returns.sort(key=lambda e: e[0])

    tr[...] = jnp.zeros(tr.shape, F32)
    low = lax.broadcasted_iota(jnp.int32, (nc, HEAD), 1) < HALF * mt
    scales = []
    for rc in range(2):
        found = list(range(rc, 2 * nc, 2))
        for i in found:
            copy = returns[i][1][0]
            copy.wait_recv() if i else copy.wait()
        stat = jnp.concatenate([rt[i] for i in found], axis=0)
        pk = stat[:, :HEAD]
        tot = pltpu.roll(pk, HALF * mt, 1) + stat[:, HEAD:]
        f = jnp.exp(jnp.minimum(pk - jnp.max(pk, axis=0, keepdims=True), 0.0))
        den = jnp.sum(jnp.where(low, f * tot, 1.0), axis=0, keepdims=True)
        tr[0:nc, :] = f / den
        scales.append(jnp.transpose(tr[...]))
    for rc in range(2):
        found = list(range(rc, 2 * nc, 2))
        source = core if rc == 0 else other
        for i in found:
            copy = returns[i][1][1]
            copy.wait_recv() if i else copy.wait()
        for c in range(HALF):
            acc = jnp.zeros((mt, HEAD), F32)
            for k, i in enumerate(found):
                acc = acc + rb[i, c].astype(F32) * scales[rc][c * mt : (c + 1) * mt, k : k + 1]
            xl[0:mt, pl.ds(pl.multiple_of(source * cols + c * HEAD, HEAD), HEAD)] = acc.astype(
                BF
            ).astype(F32)

    layer = xl[...]
    ss[...] = jnp.broadcast_to(
        jnp.sum(layer * layer, axis=1, keepdims=True) / (HEADS * HEAD), ss.shape
    )
    pre = ss[0:tokens, :]
    dec = ss[mt : mt + 1, :]
    for m in range(1, MEM):
        pre = pre + ss[m * tokens : (m + 1) * tokens, :]
        dec = dec + ss[mt + m : mt + m + 1, :]
    pre = lax.rsqrt(pre + 1e-05)
    for m in range(MEM):
        iv[m * tokens : (m + 1) * tokens, :] = pre
    iv[mt : mt + MEM, :] = jnp.broadcast_to(lax.rsqrt(dec + 1e-05), (MEM, HEAD))
    inv = iv[...]
    def xrow(slot, c):
        return pl.ds(pl.multiple_of((c * nc + slot) * bs, bs), bs)

    per = KV // PARTS
    moved = []
    for p in range(PARTS):
        block = lanes[p * per : (p + 1) * per]
        normed = jnp.concatenate([layer[:, s] * inv * gs[:, s] for s in block], axis=1).astype(BF)
        xs[p] = (
            jnp.dot(pm[...], normed, preferred_element_type=F32)
            .astype(BF)
            .reshape(EXPERTS, bs, per * HEAD)
        )
        out = {}
        for j, d in sorted(chips[1:], key=lambda jd: -(min(jd[1], EXPERTS - jd[1]) + (jd[0] > 0))):
            i = j * EXPERTS + d
            copy = remote(
                xs.at[p, lax.rem(outer + d, EXPERTS)], xg.at[p, xrow(mine, core)],
                gsend.at[p, i], grecv.at[p, i], there(j, d, core),
            )
            copy.start()
            out[j, d] = copy
        moved.append(out)
    shared = [[] for _ in range(PARTS)]
    for copy in early + list(sent.values()):
        copy.wait_send()
    for i, pair in returns:
        if i:
            for copy in pair:
                copy.wait_send()
    arrival = sorted(chips[1:], key=lambda jd: (min(jd[1], EXPERTS - jd[1]) + (jd[0] > 0)))

    def widen(p, where):
        for c in range(per):
            xf[p * per + c, where, :] = xg[p, where, lanes[c]].astype(F32)

    def first_half(p):
        where = xrow(mine, core)
        i = 2 + p * nc
        copy = remote(
            xs.at[p, outer], xg.at[p, where], psend.at[i], precv.at[i], partner
        )
        copy.start()
        shared[p].append(copy)
        xg[p, where, :] = xs[p, outer]
        widen(p, where)
        for j, d in arrival:
            moved[p][j, d].wait_recv()
            where = xrow(slot_from(j, d), core)
            i = 2 + p * nc + j * EXPERTS + d
            copy = remote(xg.at[p, where], xg.at[p, where], psend.at[i], precv.at[i], partner)
            copy.start()
            shared[p].append(copy)
            widen(p, where)

    def second_half(p):
        for copy, (j, d) in zip(shared[p], [(0, 0)] + arrival):
            copy.wait_recv()
            widen(p, xrow(slot_from(j, d), other))
        for k in range(CAP):
            for c in range(p * per, (p + 1) * per):
                for m in range(MEM):
                    i = c * MEM + m
                    x[k * n : (k + 1) * n, i * HEAD : (i + 1) * HEAD] = xf[
                        c, pl.ds(m * CAP + k, n, stride=bs), :
                    ].astype(BF)

    ff = wg_ref.shape[1]
    step = 256 if ff % 256 == 0 else ff
    steps = ff // step
    deep = per * MEM * HEAD

    def up(p, i):
        where = slice(i * step, (i + 1) * step)
        part = slice(p * deep, (p + 1) * deep)
        gated = jnp.dot(x[:, part], wg_ref[part, where], preferred_element_type=F32)
        raised = jnp.dot(x[:, part], wu_ref[part, where], preferred_element_type=F32)
        if p:
            gated = gated + ga[:, where]
            raised = raised + ua[:, where]
        if p < PARTS - 1:
            ga[:, where] = gated
            ua[:, where] = raised
        else:
            hid[:, where] = (gated / (1.0 + jnp.exp(-gated)) * raised).astype(BF)

    first_half(0)
    second_half(0)
    for load in loads[7:9]:
        load.wait()
    for p in range(PARTS):
        middle = (steps * 4) // 7 if p < PARTS - 1 else steps
        for i in range(middle):
            up(p, i)
        if p < PARTS - 1:
            first_half(p + 1)
            for i in range(middle, steps):
                up(p, i)
            second_half(p + 1)
    loads[9].wait()

    each = KV // CHUNKS
    width = each * HEAD
    far = nc * bs
    swaps = []
    outs = []

    def down(g):
        for e in range(each):
            c = g * each + e
            piece = jnp.dot(
                hid[...], wd_ref[:, c * MEM * HEAD : (c + 1) * MEM * HEAD], preferred_element_type=F32
            ).astype(BF).astype(F32)
            for k in range(CAP):
                for m in range(MEM):
                    pf[c, pl.ds(m * CAP + k, n, stride=bs), :] = piece[k * n : (k + 1) * n, lanes[m]]
            pb[g, :, lanes[e]] = pf[c, pl.ds(pl.multiple_of(other * far, far), far), :].astype(BF)
        i = 2 + PARTS * nc + g
        copy = remote(pb.at[g], p1.at[g], psend.at[i], precv.at[i], partner)
        copy.start()
        swaps.append(copy)

    def send_out(g, near):
        for o in range(EXPERTS):
            for hh in range(hs):
                if (o + hh == 0) != near:
                    continue
                d = lax.rem(o + EXPERTS - outer, EXPERTS)
                j = lax.rem(hh + hs - h, hs)
                i = j * EXPERTS + d

                @pl.when(i != 0)
                def _(o=o, hh=hh, i=i, g=g):
                    remote(
                        ys.at[g, pl.ds((hh * EXPERTS + o) * bs, bs)],
                        yr.at[g, pl.ds(pl.multiple_of(i * bs, bs), bs)],
                        ysend.at[g, i], yrecv.at[g, i], at(o, hh, core),
                    ).start()

    def deliver(g):
        swaps[g].wait_recv()
        for e in range(each):
            c = g * each + e
            ys[g, :, lanes[e]] = (
                pf[c, pl.ds(pl.multiple_of(core * far, far), far), :]
                + p1[g, :, lanes[e]].astype(F32)
            ).astype(BF)
        for i in range(1, nc):
            outs.append(
                remote(
                    ys.at[g, pl.ds(i * bs, bs)], yr.at[g, pl.ds(i * bs, bs)],
                    ysend.at[g, i], yrecv.at[g, i], partner,
                )
            )
        send_out(g, True)
        if g == CHUNKS - 1:
            send_out(g - 1, False)
        if g != CHUNKS - 2:
            send_out(g, False)
        yr[g, 0:bs, :] = ys[g, pl.ds(pl.multiple_of(mine * bs, bs), bs), :]

    for g in range(CHUNKS):
        down(g)
        if g:
            deliver(g - 1)
    deliver(CHUNKS - 1)
    each_out = nc - 1
    for copy in swaps:
        copy.wait_send()
    for p in range(PARTS):
        for copy in list(moved[p].values()) + shared[p]:
            copy.wait_send()
    for g in range(CHUNKS):
        for copy in outs[g * each_out : (g + 1) * each_out]:
            copy.wait_recv()
        where = slice(g * width, (g + 1) * width)
        osc[:, where] = (
            xl[:, where]
            + jnp.dot(gm[0], yr[g], preferred_element_type=F32)
            + jnp.dot(gm[1], yr[g], preferred_element_type=F32)
        )
        for c in range(g * each, (g + 1) * each):
            for m in range(MEM):
                i = c * MEM + m
                out_ref[0:tokens, i * HEAD : (i + 1) * HEAD] = osc[
                    m * tokens : (m + 1) * tokens, lanes[c]
                ].astype(BF)
                out_ref[tokens:rows, i * HEAD : (i + 1) * HEAD] = osc[
                    mt + m : mt + m + 1, lanes[c]
                ].astype(BF)
        for copy in outs[g * each_out : (g + 1) * each_out]:
            copy.wait_send()


def on_device(n, *args):
    (q, k, v, dq, dk, dv, dlen, idx, gate, gain, wg, wu, wd) = args
    width = q.shape[1]
    tokens = q.shape[0]
    rows = tokens + dq.shape[0]
    nc = n // 2
    ff = wg.shape[2]
    mt, bs = MEM * tokens, MEM * CAP
    side = (mt + MEM + 15) // 16 * 16
    wide = max(n * CAP, FULL)
    lanes = KV * HEAD
    hbm = pl.BlockSpec(memory_space=pl.ANY)
    vm = pl.BlockSpec(memory_space=pltpu.VMEM)
    positions = 2 * k.shape[0]
    dma = pltpu.SemaphoreType.DMA
    out = pl.pallas_call(
        functools.partial(body, n),
        out_shape=pltpu.VMEM((rows, width), BF),
        in_specs=[hbm] * 13,
        out_specs=vm,
        scratch_shapes=[
            pltpu.SMEM(dlen.shape, jnp.int32),
            pltpu.SMEM(idx.T.shape, jnp.int32),
            pltpu.SMEM(gate.T.shape, F32),
            pltpu.VMEM(q.shape, BF),
            pltpu.VMEM(dq.shape, BF),
            pltpu.VMEM((1, width), F32),
            pltpu.VMEM((positions, HALF * HEAD), BF),
            pltpu.VMEM((positions, HALF * HEAD), BF),
            pltpu.VMEM(dk.shape[1:], BF),
            pltpu.VMEM(dv.shape[1:], BF),
            pltpu.VMEM(wg.shape[1:], BF),
            pltpu.VMEM(wu.shape[1:], BF),
            pltpu.VMEM(wd.shape[1:], BF),
            pltpu.VMEM((KV, mt, HEAD), F32),
            pltpu.VMEM((2, HALF, mt, HEAD), BF),
            pltpu.VMEM((HALF, nc * 2 * mt, HEAD), BF),
            pltpu.VMEM((n, HALF, mt, HEAD), BF),
            pltpu.VMEM((n, HALF, mt, HEAD), BF),
            pltpu.VMEM((n, 1, 2 * HEAD), F32),
            pltpu.VMEM((n, 1, 2 * HEAD), F32),
            pltpu.VMEM((HEAD, HEAD), F32),
            pltpu.VMEM((HEADS, HEAD), F32),
            pltpu.VMEM((side, lanes), F32),
            pltpu.VMEM((side, lanes), F32),
            pltpu.VMEM((side, HEAD), F32),
            pltpu.VMEM((side, HEAD), F32),
            pltpu.VMEM((EXPERTS * bs, side), BF),
            pltpu.VMEM((2, side, nc * bs), BF),
            pltpu.VMEM((PARTS, EXPERTS, bs, lanes // PARTS), BF),
            pltpu.VMEM((PARTS, n * bs, lanes // PARTS), BF),
            pltpu.VMEM((KV, n * bs, HEAD), F32),
            pltpu.VMEM((wide, width), BF),
            pltpu.VMEM((wide, ff), F32),
            pltpu.VMEM((wide, ff), F32),
            pltpu.VMEM((wide, ff), BF),
            pltpu.VMEM((KV, n * bs, HEAD), F32),
            pltpu.VMEM((CHUNKS, nc * bs, lanes // CHUNKS), BF),
            pltpu.VMEM((CHUNKS, nc * bs, lanes // CHUNKS), BF),
            pltpu.VMEM((CHUNKS, nc * bs, lanes // CHUNKS), BF),
            pltpu.VMEM((CHUNKS, nc * bs, lanes // CHUNKS), BF),
            pltpu.VMEM((side, lanes), F32),
            dma((n,)),
            dma((n,)),
            dma((PARTS, nc)),
            dma((PARTS, nc)),
            dma((n,)),
            dma((n,)),
            dma((n,)),
            dma((n,)),
            dma((2 + PARTS * nc + CHUNKS,)),
            dma((2 + PARTS * nc + CHUNKS,)),
            dma((CHUNKS, nc)),
            dma((CHUNKS, nc)),
            dma((13,)),
        ],
        compiler_params=pltpu.CompilerParams(
            collective_id=0, has_side_effects=True, vmem_limit_bytes=60_000_000
        ),
        name="moe_layer",
    )(q, dq, dlen, idx.T, gate.T, gain[None], k, v, dk, dv, wg, wu, wd)
    return out[:tokens], out[tokens:]


def solution(mesh):
    both = ("groups", "seq")
    in_specs = (
        P(both, None),
        P(both, None),
        P(both, None),
        P(both, None),
        P(both, None, None),
        P(both, None, None),
        P(both),
        P(both, None),
        P(both, None),
        P(),
        P("seq", None, None),
        P("seq", None, None),
        P("seq", None, None),
    )
    return jax.shard_map(
        functools.partial(on_device, mesh.shape["seq"]),
        mesh=mesh,
        in_specs=in_specs,
        out_specs=(P(both, None), P(both, None)),
        check_vma=False,
    )
```

```python
import functools

import jax
import jax.numpy as jnp
from jax import lax
from jax.experimental import pallas as pl
from jax.experimental.pallas import tpu as pltpu
from jax.sharding import PartitionSpec as P

HEADS = 32
KV = 8
MEM = HEADS // KV
HEAD = 128
EXPERTS = 4
CAP = 4
HALF = KV // 2
F32 = jnp.float32
BF = jnp.bfloat16
CHUNKS = 4
FULL = 128
PARTS = 2
MESH = pl.DeviceIdType.MESH


def body(
    n,
    q_hbm,
    dq_hbm,
    len_hbm,
    idx_hbm,
    gate_hbm,
    gain_hbm,
    k_hbm,
    v_hbm,
    dk_hbm,
    dv_hbm,
    wg_hbm,
    wu_hbm,
    wd_hbm,
    out_ref,
    len_ref,
    idx_ref,
    gate_ref,
    q_ref,
    dq_ref,
    gain_ref,
    k_ref,
    v_ref,
    dk_ref,
    dv_ref,
    wg_ref,
    wu_ref,
    wd_ref,
    qs,
    qh,
    qg,
    sb,
    rb,
    st,
    rt,
    tr,
    dqs,
    gs,
    xl,
    ss,
    iv,
    pm,
    gm,
    xs,
    xg,
    xf,
    x,
    ga,
    ua,
    hid,
    pf,
    pb,
    p1,
    ys,
    yr,
    osc,
    qsend,
    qrecv,
    gsend,
    grecv,
    rsend,
    rrecv,
    tsend,
    trecv,
    psend,
    precv,
    ysend,
    yrecv,
    local,
):
    hs = n // (2 * EXPERTS)
    nc = hs * EXPERTS
    me = lax.axis_index("seq")
    core = lax.rem(me, 2)
    h = lax.rem(me // 2, hs)
    outer = me // (2 * hs)
    other = 1 - core

    def at(o, hh, c):
        return {"seq": (o * hs + hh) * 2 + c}

    def there(j, d, c):
        return at(lax.rem(outer + d, EXPERTS), lax.rem(h + j, hs), c)

    def slot_to(j, d):
        return lax.rem(h + j, hs) * EXPERTS + lax.rem(outer + d, EXPERTS)

    def slot_from(j, d):
        return lax.rem(h + hs - j, hs) * EXPERTS + lax.rem(outer + EXPERTS - d, EXPERTS)

    partner = at(outer, h, other)
    mine = h * EXPERTS + outer
    chips = [(j, d) for j in range(hs) for d in range(EXPERTS)]
    barrier = pltpu.get_barrier_semaphore()
    for j, d in chips:
        for c in (core, other):
            if (j, d) != (0, 0) or c is other:
                pl.semaphore_signal(barrier, inc=1, device_id=there(j, d, c), device_id_type=MESH)

    length = k_ref.shape[0] // 2
    cols = HALF * HEAD

    def half(c):
        return pl.ds(pl.multiple_of(c * cols, cols), cols)

    sources = [
        (q_hbm, q_ref),
        (dq_hbm, dq_ref),
        (gain_hbm, gain_ref),
        (dk_hbm.at[0], dk_ref),
        (dv_hbm.at[0], dv_ref),
        (k_hbm.at[:, half(core)], k_ref.at[pl.ds(0, length)]),
        (v_hbm.at[:, half(core)], v_ref.at[pl.ds(0, length)]),
        (wg_hbm.at[0], wg_ref),
        (wu_hbm.at[0], wu_ref),
        (wd_hbm.at[0], wd_ref),
        (len_hbm, len_ref),
        (idx_hbm, idx_ref),
        (gate_hbm, gate_ref),
    ]
    loads = [pltpu.make_async_copy(s, t, local.at[i]) for i, (s, t) in enumerate(sources)]
    for load in loads[:3] + loads[10:] + loads[3:7]:
        load.start()

    def remote(src, dst, ssem, rsem, peer):
        return pltpu.make_async_remote_copy(
            src_ref=src, dst_ref=dst, send_sem=ssem, recv_sem=rsem,
            device_id=peer, device_id_type=MESH,
        )

    tokens = q_ref.shape[0]
    rows = tokens + 1
    mt = MEM * tokens
    bs = MEM * CAP
    lanes = [slice(c * HEAD, (c + 1) * HEAD) for c in range(KV)]

    loads[0].wait()
    wide = q_ref[...].astype(F32)
    for c in range(KV):
        for m in range(MEM):
            i = c * MEM + m
            qs[c, m * tokens : (m + 1) * tokens, :] = wide[:, i * HEAD : (i + 1) * HEAD]
    for c in range(2):
        qh[c] = qs[c * HALF : (c + 1) * HALF].astype(BF)

    pl.semaphore_wait(barrier, n - 1)
    early = [
        remote(k_hbm.at[:, half(other)], k_ref.at[pl.ds(length, length)], psend.at[0], precv.at[0], partner),
        remote(v_hbm.at[:, half(other)], v_ref.at[pl.ds(length, length)], psend.at[1], precv.at[1], partner),
    ]
    qrows = 2 * mt

    def qslot(slot, count=1):
        return pl.ds(pl.multiple_of(slot * qrows, qrows), count * qrows)

    here = pl.ds(pl.multiple_of(mine * qrows + core * mt, mt), mt)
    sent = {}
    for j, d in chips:
        for rc in range(2):
            to = core if rc == 0 else other
            i = (j * EXPERTS + d) * 2 + rc
            if i:
                copy = remote(
                    qh.at[to], qg.at[:, here], qsend.at[i], qrecv.at[i], there(j, d, to)
                )
                copy.start()
                sent[i] = copy
    qg[:, here, :] = qh[core]
    for copy in early:
        copy.start()
    for load in loads[7:10]:
        load.start()
    for load in loads[10:]:
        load.wait()

    spots = []
    for r in range(rows):
        for t in range(idx_ref.shape[0]):
            named = idx_ref[t, r]
            spot = jnp.int32(0)
            for before in range(r):
                hit = (idx_ref[0, before] == named) | (idx_ref[1, before] == named)
                spot = spot + jnp.where(hit, 1, 0)
            spots.append((r, named, spot, gate_ref[t, r]))

    def token_of(i):
        return jnp.where(i < mt, lax.rem(i, tokens), jnp.where(i < mt + MEM, tokens, rows))

    def member_of(i):
        return jnp.where(i < mt, i // tokens, i - mt)

    side = xl.shape[0]
    a = lax.broadcasted_iota(jnp.int32, (EXPERTS * bs, side), 0)
    b = lax.broadcasted_iota(jnp.int32, (EXPERTS * bs, side), 1)
    same = lax.rem(a, bs) // CAP == member_of(b)
    pick = jnp.zeros((EXPERTS * bs, side), F32)
    code = a // bs * CAP + lax.rem(a, CAP)
    tok = jnp.where(same, token_of(b), rows)
    for r, named, spot, _ in spots:
        pick = jnp.where((tok == r) & (code == named * CAP + spot), 1.0, pick)
    pm[...] = pick.astype(BF)
    a = lax.broadcasted_iota(jnp.int32, (side, nc * bs), 0)
    b = lax.broadcasted_iota(jnp.int32, (side, nc * bs), 1)
    same = lax.rem(b, bs) // CAP == member_of(a)
    tok = jnp.where(same, token_of(a), rows)
    expert = lax.rem(outer + EXPERTS - lax.rem(b // bs, EXPERTS), EXPERTS)
    code = expert * CAP + lax.rem(b, CAP)
    mix = jnp.zeros((side, nc * bs), F32)
    for r, named, spot, gate in spots:
        mix = jnp.where((tok == r) & (code == named * CAP + spot), gate, mix)
    high = mix.astype(BF)
    gm[0] = high
    gm[1] = (mix - high.astype(F32)).astype(BF)

    scale = HEAD ** (-0.5)
    if x.shape[0] > n * CAP:
        x[n * CAP :, :] = jnp.zeros((x.shape[0] - n * CAP, x.shape[1]), BF)
    xl[...] = jnp.zeros(xl.shape, F32)
    iv[...] = jnp.zeros(iv.shape, F32)
    gs[...] = jnp.zeros(gs.shape, F32)
    loads[1].wait()
    loads[2].wait()
    wide = dq_ref[...].astype(F32)
    for c in range(KV):
        for m in range(MEM):
            i = c * MEM + m
            gain = gain_ref[:, i * HEAD : (i + 1) * HEAD]
            dqs[i : i + 1, :] = wide[:, i * HEAD : (i + 1) * HEAD]
            gs[m * tokens : (m + 1) * tokens, lanes[c]] = jnp.broadcast_to(gain, (tokens, HEAD))
            gs[mt + m : mt + m + 1, lanes[c]] = gain
    dq = dqs[...].astype(BF)
    dlen = dk_ref.shape[0]
    loads[3].wait()
    head_of = lax.broadcasted_iota(jnp.int32, (HEADS, dlen), 0) // MEM
    scores = jnp.zeros((HEADS, dlen), F32)
    for c in range(KV):
        part = lax.dot_general(
            dq, dk_ref[:, lanes[c]], (((1,), (1,)), ((), ())), preferred_element_type=F32
        )
        scores = jnp.where(head_of == c, part, scores)
    scores = scores * scale
    live = lax.broadcasted_iota(jnp.int32, (HEADS, dlen), 1) < len_ref[0]
    scores = jnp.where(live, scores, -1e30)
    peak = jnp.max(scores, axis=-1, keepdims=True)
    weights = jnp.where(live, jnp.exp(scores - peak), 0.0)
    total = jnp.sum(weights, axis=-1, keepdims=True)
    loads[4].wait()
    acc = jnp.zeros((HEADS, HEAD), F32)
    for c in range(KV):
        masked = jnp.where(head_of == c, weights, 0.0).astype(BF)
        acc = acc + jnp.dot(masked, dv_ref[:, lanes[c]], preferred_element_type=F32)
    dqs[...] = (acc / total).astype(BF).astype(F32)
    for c in range(KV):
        xl[mt : mt + MEM, lanes[c]] = dqs[c * MEM : (c + 1) * MEM, :]

    loads[5].wait()
    loads[6].wait()
    for copy in early:
        copy.wait_recv()
    returns = []
    count = EXPERTS * qrows
    a = lax.broadcasted_iota(jnp.int32, (HEAD, 2 * HEAD), 0)
    b = lax.broadcasted_iota(jnp.int32, (HEAD, 2 * HEAD), 1)
    spread = jnp.where(a == b // mt, 1.0, 0.0).astype(BF)
    a = lax.broadcasted_iota(jnp.int32, (count, 2 * HEAD), 0)
    b = lax.broadcasted_iota(jnp.int32, (count, 2 * HEAD), 1)
    sel = lax.rem(a, mt) == lax.rem(b, mt)
    lane = lax.broadcasted_iota(jnp.int32, (count, HEAD), 1)
    for j in range(hs):
        for i in range(j * EXPERTS * 2, (j + 1) * EXPERTS * 2):
            if i:
                sent[i].wait_recv()
        group = lax.rem(h + hs - j, hs)
        stats = jnp.zeros((count, HEAD), F32)
        first = pl.multiple_of(group * EXPERTS * 2, EXPERTS * 2)
        for c in range(HALF):
            sc = lax.dot_general(
                qg[c, qslot(group * EXPERTS, EXPERTS), :], k_ref[:, lanes[c]],
                (((1,), (1,)), ((), ())), preferred_element_type=F32,
            ) * scale
            pk = jnp.max(sc, axis=-1, keepdims=True).astype(BF).astype(F32)
            w = jnp.exp(sc - pk)
            tot = jnp.sum(w, axis=-1, keepdims=True)
            num = jnp.dot(w.astype(BF), v_ref[:, lanes[c]], preferred_element_type=F32)
            sb[pl.ds(first, EXPERTS * 2), c] = num.astype(BF).reshape(EXPERTS * 2, mt, HEAD)
            tot_high = tot.astype(BF).astype(F32)
            stats = jnp.where(lane == c, pk, stats)
            stats = jnp.where(lane == HALF + c, tot_high, stats)
            stats = jnp.where(lane == 2 * HALF + c, tot - tot_high, stats)
        compact = jnp.where(
            sel, jnp.dot(stats.astype(BF), spread, preferred_element_type=F32), 0.0
        )
        compact = jnp.sum(compact.reshape(EXPERTS * 2, mt, 2 * HEAD), axis=1)
        for i in range(EXPERTS * 2):
            st[first + i] = compact[i : i + 1]
        jj = (hs - j) % hs
        for d in sorted(range(EXPERTS), key=lambda d: -min(d, EXPERTS - d)):
            for rc in range(2):
                to = core if rc == 0 else other
                slot = slot_to(jj, d) * 2 + to
                i = (jj * EXPERTS + d) * 2 + rc
                pair = []
                for src, dst, ssem, rsem in (
                    (st.at[slot], rt.at[i], tsend.at[i], trecv.at[i]),
                    (sb.at[slot], rb.at[i], rsend.at[i], rrecv.at[i]),
                ):
                    if i == 0:
                        copy = pltpu.make_async_copy(src, dst, rsem)
                    else:
                        copy = remote(src, dst, ssem, rsem, there(jj, d, to))
                    copy.start()
                    pair.append(copy)
                returns.append((i, pair))
    returns.sort(key=lambda e: e[0])

    tr[...] = jnp.zeros(tr.shape, F32)
    low = lax.broadcasted_iota(jnp.int32, (nc, HEAD), 1) < HALF * mt
    scales = []
    for rc in range(2):
        found = list(range(rc, 2 * nc, 2))
        for i in found:
            copy = returns[i][1][0]
            copy.wait_recv() if i else copy.wait()
        stat = jnp.concatenate([rt[i] for i in found], axis=0)
        pk = stat[:, :HEAD]
        tot = pltpu.roll(pk, HALF * mt, 1) + stat[:, HEAD:]
        f = jnp.exp(jnp.minimum(pk - jnp.max(pk, axis=0, keepdims=True), 0.0))
        den = jnp.sum(jnp.where(low, f * tot, 1.0), axis=0, keepdims=True)
        tr[0:nc, :] = f / den
        scales.append(jnp.transpose(tr[...]))
    for rc in range(2):
        found = list(range(rc, 2 * nc, 2))
        source = core if rc == 0 else other
        for i in found:
            copy = returns[i][1][1]
            copy.wait_recv() if i else copy.wait()
        for c in range(HALF):
            acc = jnp.zeros((mt, HEAD), F32)
            for k, i in enumerate(found):
                acc = acc + rb[i, c].astype(F32) * scales[rc][c * mt : (c + 1) * mt, k : k + 1]
            xl[0:mt, pl.ds(pl.multiple_of(source * cols + c * HEAD, HEAD), HEAD)] = acc.astype(
                BF
            ).astype(F32)

    layer = xl[...]
    ss[...] = jnp.broadcast_to(
        jnp.sum(layer * layer, axis=1, keepdims=True) / (HEADS * HEAD), ss.shape
    )
    pre = ss[0:tokens, :]
    dec = ss[mt : mt + 1, :]
    for m in range(1, MEM):
        pre = pre + ss[m * tokens : (m + 1) * tokens, :]
        dec = dec + ss[mt + m : mt + m + 1, :]
    pre = lax.rsqrt(pre + 1e-05)
    for m in range(MEM):
        iv[m * tokens : (m + 1) * tokens, :] = pre
    iv[mt : mt + MEM, :] = jnp.broadcast_to(lax.rsqrt(dec + 1e-05), (MEM, HEAD))
    inv = iv[...]
    def xrow(slot, c):
        return pl.ds(pl.multiple_of((c * nc + slot) * bs, bs), bs)

    per = KV // PARTS
    moved = []
    for p in range(PARTS):
        block = lanes[p * per : (p + 1) * per]
        normed = jnp.concatenate([layer[:, s] * inv * gs[:, s] for s in block], axis=1).astype(BF)
        xs[p] = (
            jnp.dot(pm[...], normed, preferred_element_type=F32)
            .astype(BF)
            .reshape(EXPERTS, bs, per * HEAD)
        )
        out = {}
        for j, d in sorted(chips[1:], key=lambda jd: -(min(jd[1], EXPERTS - jd[1]) + (jd[0] > 0))):
            i = j * EXPERTS + d
            copy = remote(
                xs.at[p, lax.rem(outer + d, EXPERTS)], xg.at[p, xrow(mine, core)],
                gsend.at[p, i], grecv.at[p, i], there(j, d, core),
            )
            copy.start()
            out[j, d] = copy
        moved.append(out)
    shared = [[] for _ in range(PARTS)]
    for copy in early + list(sent.values()):
        copy.wait_send()
    for i, pair in returns:
        if i:
            for copy in pair:
                copy.wait_send()
    arrival = sorted(chips[1:], key=lambda jd: (min(jd[1], EXPERTS - jd[1]) + (jd[0] > 0)))

    def widen(p, where):
        for c in range(per):
            xf[p * per + c, where, :] = xg[p, where, lanes[c]].astype(F32)

    def first_half(p):
        where = xrow(mine, core)
        i = 2 + p * nc
        copy = remote(
            xs.at[p, outer], xg.at[p, where], psend.at[i], precv.at[i], partner
        )
        copy.start()
        shared[p].append(copy)
        xg[p, where, :] = xs[p, outer]
        widen(p, where)
        for j, d in arrival:
            moved[p][j, d].wait_recv()
            where = xrow(slot_from(j, d), core)
            i = 2 + p * nc + j * EXPERTS + d
            copy = remote(xg.at[p, where], xg.at[p, where], psend.at[i], precv.at[i], partner)
            copy.start()
            shared[p].append(copy)
            widen(p, where)

    def second_half(p):
        for copy, (j, d) in zip(shared[p], [(0, 0)] + arrival):
            copy.wait_recv()
            widen(p, xrow(slot_from(j, d), other))
        for k in range(CAP):
            for c in range(p * per, (p + 1) * per):
                for m in range(MEM):
                    i = c * MEM + m
                    x[k * n : (k + 1) * n, i * HEAD : (i + 1) * HEAD] = xf[
                        c, pl.ds(m * CAP + k, n, stride=bs), :
                    ].astype(BF)

    ff = wg_ref.shape[1]
    step = 256 if ff % 256 == 0 else ff
    steps = ff // step
    deep = per * MEM * HEAD

    def up(p, i):
        where = slice(i * step, (i + 1) * step)
        part = slice(p * deep, (p + 1) * deep)
        gated = jnp.dot(x[:, part], wg_ref[part, where], preferred_element_type=F32)
        raised = jnp.dot(x[:, part], wu_ref[part, where], preferred_element_type=F32)
        if p:
            gated = gated + ga[:, where]
            raised = raised + ua[:, where]
        if p < PARTS - 1:
            ga[:, where] = gated
            ua[:, where] = raised
        else:
            hid[:, where] = (gated / (1.0 + jnp.exp(-gated)) * raised).astype(BF)

    first_half(0)
    second_half(0)
    for load in loads[7:9]:
        load.wait()
    for p in range(PARTS):
        middle = (steps * 4) // 7 if p < PARTS - 1 else steps
        for i in range(middle):
            up(p, i)
        if p < PARTS - 1:
            first_half(p + 1)
            for i in range(middle, steps):
                up(p, i)
            second_half(p + 1)
    loads[9].wait()

    each = KV // CHUNKS
    width = each * HEAD
    far = nc * bs
    swaps = []
    outs = []

    def down(g):
        for e in range(each):
            c = g * each + e
            piece = jnp.dot(
                hid[...], wd_ref[:, c * MEM * HEAD : (c + 1) * MEM * HEAD], preferred_element_type=F32
            )[: n * CAP].astype(BF).astype(F32)
            for k in range(CAP):
                for m in range(MEM):
                    pf[c, pl.ds(m * CAP + k, n, stride=bs), :] = piece[k * n : (k + 1) * n, lanes[m]]
            pb[g, :, lanes[e]] = pf[c, pl.ds(pl.multiple_of(other * far, far), far), :].astype(BF)
        i = 2 + PARTS * nc + g
        copy = remote(pb.at[g], p1.at[g], psend.at[i], precv.at[i], partner)
        copy.start()
        swaps.append(copy)

    def send_out(g, near):
        for o in range(EXPERTS):
            for hh in range(hs):
                if (o + hh == 0) != near:
                    continue
                d = lax.rem(o + EXPERTS - outer, EXPERTS)
                j = lax.rem(hh + hs - h, hs)
                i = j * EXPERTS + d

                @pl.when(i != 0)
                def _(o=o, hh=hh, i=i, g=g):
                    remote(
                        ys.at[g, pl.ds((hh * EXPERTS + o) * bs, bs)],
                        yr.at[g, pl.ds(pl.multiple_of(i * bs, bs), bs)],
                        ysend.at[g, i], yrecv.at[g, i], at(o, hh, core),
                    ).start()

    def deliver(g):
        swaps[g].wait_recv()
        for e in range(each):
            c = g * each + e
            ys[g, :, lanes[e]] = (
                pf[c, pl.ds(pl.multiple_of(core * far, far), far), :]
                + p1[g, :, lanes[e]].astype(F32)
            ).astype(BF)
        for i in range(1, nc):
            outs.append(
                remote(
                    ys.at[g, pl.ds(i * bs, bs)], yr.at[g, pl.ds(i * bs, bs)],
                    ysend.at[g, i], yrecv.at[g, i], partner,
                )
            )
        send_out(g, True)
        if g == CHUNKS - 1:
            for late in range(1, CHUNKS):
                send_out(late, False)
        if g == 0:
            send_out(g, False)
        yr[g, 0:bs, :] = ys[g, pl.ds(pl.multiple_of(mine * bs, bs), bs), :]

    for g in range(CHUNKS):
        down(g)
        if g:
            deliver(g - 1)
    deliver(CHUNKS - 1)
    each_out = nc - 1
    for copy in swaps:
        copy.wait_send()
    for p in range(PARTS):
        for copy in list(moved[p].values()) + shared[p]:
            copy.wait_send()
    for g in range(CHUNKS):
        for copy in outs[g * each_out : (g + 1) * each_out]:
            copy.wait_recv()
        where = slice(g * width, (g + 1) * width)
        osc[:, where] = (
            xl[:, where]
            + jnp.dot(gm[0], yr[g], preferred_element_type=F32)
            + jnp.dot(gm[1], yr[g], preferred_element_type=F32)
        )
        for c in range(g * each, (g + 1) * each):
            for m in range(MEM):
                i = c * MEM + m
                out_ref[0:tokens, i * HEAD : (i + 1) * HEAD] = osc[
                    m * tokens : (m + 1) * tokens, lanes[c]
                ].astype(BF)
                out_ref[tokens:rows, i * HEAD : (i + 1) * HEAD] = osc[
                    mt + m : mt + m + 1, lanes[c]
                ].astype(BF)
        for copy in outs[g * each_out : (g + 1) * each_out]:
            copy.wait_send()


def on_device(n, *args):
    (q, k, v, dq, dk, dv, dlen, idx, gate, gain, wg, wu, wd) = args
    width = q.shape[1]
    tokens = q.shape[0]
    rows = tokens + dq.shape[0]
    nc = n // 2
    ff = wg.shape[2]
    mt, bs = MEM * tokens, MEM * CAP
    side = (mt + MEM + 15) // 16 * 16
    wide = max(n * CAP, FULL)
    lanes = KV * HEAD
    hbm = pl.BlockSpec(memory_space=pl.ANY)
    vm = pl.BlockSpec(memory_space=pltpu.VMEM)
    positions = 2 * k.shape[0]
    dma = pltpu.SemaphoreType.DMA
    out = pl.pallas_call(
        functools.partial(body, n),
        out_shape=pltpu.VMEM((rows, width), BF),
        in_specs=[hbm] * 13,
        out_specs=vm,
        scratch_shapes=[
            pltpu.SMEM(dlen.shape, jnp.int32),
            pltpu.SMEM(idx.T.shape, jnp.int32),
            pltpu.SMEM(gate.T.shape, F32),
            pltpu.VMEM(q.shape, BF),
            pltpu.VMEM(dq.shape, BF),
            pltpu.VMEM((1, width), F32),
            pltpu.VMEM((positions, HALF * HEAD), BF),
            pltpu.VMEM((positions, HALF * HEAD), BF),
            pltpu.VMEM(dk.shape[1:], BF),
            pltpu.VMEM(dv.shape[1:], BF),
            pltpu.VMEM(wg.shape[1:], BF),
            pltpu.VMEM(wu.shape[1:], BF),
            pltpu.VMEM(wd.shape[1:], BF),
            pltpu.VMEM((KV, mt, HEAD), F32),
            pltpu.VMEM((2, HALF, mt, HEAD), BF),
            pltpu.VMEM((HALF, nc * 2 * mt, HEAD), BF),
            pltpu.VMEM((n, HALF, mt, HEAD), BF),
            pltpu.VMEM((n, HALF, mt, HEAD), BF),
            pltpu.VMEM((n, 1, 2 * HEAD), F32),
            pltpu.VMEM((n, 1, 2 * HEAD), F32),
            pltpu.VMEM((HEAD, HEAD), F32),
            pltpu.VMEM((HEADS, HEAD), F32),
            pltpu.VMEM((side, lanes), F32),
            pltpu.VMEM((side, lanes), F32),
            pltpu.VMEM((side, HEAD), F32),
            pltpu.VMEM((side, HEAD), F32),
            pltpu.VMEM((EXPERTS * bs, side), BF),
            pltpu.VMEM((2, side, nc * bs), BF),
            pltpu.VMEM((PARTS, EXPERTS, bs, lanes // PARTS), BF),
            pltpu.VMEM((PARTS, n * bs, lanes // PARTS), BF),
            pltpu.VMEM((KV, n * bs, HEAD), F32),
            pltpu.VMEM((wide, width), BF),
            pltpu.VMEM((wide, ff), F32),
            pltpu.VMEM((wide, ff), F32),
            pltpu.VMEM((wide, ff), BF),
            pltpu.VMEM((KV, n * bs, HEAD), F32),
            pltpu.VMEM((CHUNKS, nc * bs, lanes // CHUNKS), BF),
            pltpu.VMEM((CHUNKS, nc * bs, lanes // CHUNKS), BF),
            pltpu.VMEM((CHUNKS, nc * bs, lanes // CHUNKS), BF),
            pltpu.VMEM((CHUNKS, nc * bs, lanes // CHUNKS), BF),
            pltpu.VMEM((side, lanes), F32),
            dma((n,)),
            dma((n,)),
            dma((PARTS, nc)),
            dma((PARTS, nc)),
            dma((n,)),
            dma((n,)),
            dma((n,)),
            dma((n,)),
            dma((2 + PARTS * nc + CHUNKS,)),
            dma((2 + PARTS * nc + CHUNKS,)),
            dma((CHUNKS, nc)),
            dma((CHUNKS, nc)),
            dma((13,)),
        ],
        compiler_params=pltpu.CompilerParams(
            collective_id=0, has_side_effects=True, vmem_limit_bytes=60_000_000
        ),
        name="moe_layer",
    )(q, dq, dlen, idx.T, gate.T, gain[None], k, v, dk, dv, wg, wu, wd)
    return out[:tokens], out[tokens:]


def solution(mesh):
    both = ("groups", "seq")
    in_specs = (
        P(both, None),
        P(both, None),
        P(both, None),
        P(both, None),
        P(both, None, None),
        P(both, None, None),
        P(both),
        P(both, None),
        P(both, None),
        P(),
        P("seq", None, None),
        P("seq", None, None),
        P("seq", None, None),
    )
    return jax.shard_map(
        functools.partial(on_device, mesh.shape["seq"]),
        mesh=mesh,
        in_specs=in_specs,
        out_specs=(P(both, None), P(both, None)),
        check_vma=False,
    )
```

```python
import functools

import jax
import jax.numpy as jnp
from jax import lax
from jax.experimental import pallas as pl
from jax.experimental.pallas import tpu as pltpu
from jax.sharding import PartitionSpec as P

HEADS = 32
KV = 8
MEM = HEADS // KV
HEAD = 128
EXPERTS = 4
CAP = 4
HALF = KV // 2
F32 = jnp.float32
BF = jnp.bfloat16
CHUNKS = 4
FULL = 128
PARTS = 2
MESH = pl.DeviceIdType.MESH


def body(
    n,
    q_hbm,
    dq_hbm,
    len_hbm,
    idx_hbm,
    gate_hbm,
    gain_hbm,
    k_hbm,
    v_hbm,
    dk_hbm,
    dv_hbm,
    wg_hbm,
    wu_hbm,
    wd_hbm,
    out_ref,
    len_ref,
    idx_ref,
    gate_ref,
    q_ref,
    dq_ref,
    gain_ref,
    k_ref,
    v_ref,
    dk_ref,
    dv_ref,
    wg_ref,
    wu_ref,
    wd_ref,
    qs,
    qh,
    qg,
    sb,
    rb,
    st,
    rt,
    tr,
    dqs,
    gs,
    xl,
    ss,
    iv,
    pm,
    gm,
    xs,
    xg,
    xf,
    x,
    ga,
    ua,
    hid,
    pf,
    pb,
    p1,
    ys,
    yr,
    osc,
    qsend,
    qrecv,
    gsend,
    grecv,
    rsend,
    rrecv,
    tsend,
    trecv,
    psend,
    precv,
    ysend,
    yrecv,
    local,
):
    hs = n // (2 * EXPERTS)
    nc = hs * EXPERTS
    me = lax.axis_index("seq")
    core = lax.rem(me, 2)
    h = lax.rem(me // 2, hs)
    outer = me // (2 * hs)
    other = 1 - core

    def at(o, hh, c):
        return {"seq": (o * hs + hh) * 2 + c}

    def there(j, d, c):
        return at(lax.rem(outer + d, EXPERTS), lax.rem(h + j, hs), c)

    def slot_to(j, d):
        return lax.rem(h + j, hs) * EXPERTS + lax.rem(outer + d, EXPERTS)

    def slot_from(j, d):
        return lax.rem(h + hs - j, hs) * EXPERTS + lax.rem(outer + EXPERTS - d, EXPERTS)

    partner = at(outer, h, other)
    mine = h * EXPERTS + outer
    chips = [(j, d) for j in range(hs) for d in range(EXPERTS)]
    barrier = pltpu.get_barrier_semaphore()
    for j, d in chips:
        for c in (core, other):
            if (j, d) != (0, 0) or c is other:
                pl.semaphore_signal(barrier, inc=1, device_id=there(j, d, c), device_id_type=MESH)

    length = k_ref.shape[0] // 2
    cols = HALF * HEAD

    def half(c):
        return pl.ds(pl.multiple_of(c * cols, cols), cols)

    sources = [
        (q_hbm, q_ref),
        (dq_hbm, dq_ref),
        (gain_hbm, gain_ref),
        (dk_hbm.at[0], dk_ref),
        (dv_hbm.at[0], dv_ref),
        (k_hbm.at[:, half(core)], k_ref.at[pl.ds(0, length)]),
        (v_hbm.at[:, half(core)], v_ref.at[pl.ds(0, length)]),
        (wg_hbm.at[0], wg_ref),
        (wu_hbm.at[0], wu_ref),
        (wd_hbm.at[0], wd_ref),
        (len_hbm, len_ref),
        (idx_hbm, idx_ref),
        (gate_hbm, gate_ref),
    ]
    loads = [pltpu.make_async_copy(s, t, local.at[i]) for i, (s, t) in enumerate(sources)]
    for load in loads[:3] + loads[10:] + loads[3:7]:
        load.start()

    def remote(src, dst, ssem, rsem, peer):
        return pltpu.make_async_remote_copy(
            src_ref=src, dst_ref=dst, send_sem=ssem, recv_sem=rsem,
            device_id=peer, device_id_type=MESH,
        )

    tokens = q_ref.shape[0]
    rows = tokens + 1
    mt = MEM * tokens
    bs = MEM * CAP
    lanes = [slice(c * HEAD, (c + 1) * HEAD) for c in range(KV)]

    loads[0].wait()
    wide = q_ref[...].astype(F32)
    for c in range(KV):
        for m in range(MEM):
            i = c * MEM + m
            qs[c, m * tokens : (m + 1) * tokens, :] = wide[:, i * HEAD : (i + 1) * HEAD]
    for c in range(2):
        qh[c] = qs[c * HALF : (c + 1) * HALF].astype(BF)

    pl.semaphore_wait(barrier, n - 1)
    early = [
        remote(k_hbm.at[:, half(other)], k_ref.at[pl.ds(length, length)], psend.at[0], precv.at[0], partner),
        remote(v_hbm.at[:, half(other)], v_ref.at[pl.ds(length, length)], psend.at[1], precv.at[1], partner),
    ]
    qrows = 2 * mt

    def qslot(slot, count=1):
        return pl.ds(pl.multiple_of(slot * qrows, qrows), count * qrows)

    here = pl.ds(pl.multiple_of(mine * qrows + core * mt, mt), mt)
    sent = {}
    for j, d in chips:
        for rc in range(2):
            to = core if rc == 0 else other
            i = (j * EXPERTS + d) * 2 + rc
            if i:
                copy = remote(
                    qh.at[to], qg.at[:, here], qsend.at[i], qrecv.at[i], there(j, d, to)
                )
                copy.start()
                sent[i] = copy
    qg[:, here, :] = qh[core]
    for copy in early:
        copy.start()
    for load in loads[7:10]:
        load.start()
    for load in loads[10:]:
        load.wait()

    spots = []
    for r in range(rows):
        for t in range(idx_ref.shape[0]):
            named = idx_ref[t, r]
            spot = jnp.int32(0)
            for before in range(r):
                hit = (idx_ref[0, before] == named) | (idx_ref[1, before] == named)
                spot = spot + jnp.where(hit, 1, 0)
            spots.append((r, named, spot, gate_ref[t, r]))

    def token_of(i):
        return jnp.where(i < mt, lax.rem(i, tokens), jnp.where(i < mt + MEM, tokens, rows))

    def member_of(i):
        return jnp.where(i < mt, i // tokens, i - mt)

    side = xl.shape[0]
    a = lax.broadcasted_iota(jnp.int32, (EXPERTS * bs, side), 0)
    b = lax.broadcasted_iota(jnp.int32, (EXPERTS * bs, side), 1)
    same = lax.rem(a, bs) // CAP == member_of(b)
    pick = jnp.zeros((EXPERTS * bs, side), F32)
    code = a // bs * CAP + lax.rem(a, CAP)
    tok = jnp.where(same, token_of(b), rows)
    for r, named, spot, _ in spots:
        pick = jnp.where((tok == r) & (code == named * CAP + spot), 1.0, pick)
    pm[...] = pick.astype(BF)
    a = lax.broadcasted_iota(jnp.int32, (side, nc * bs), 0)
    b = lax.broadcasted_iota(jnp.int32, (side, nc * bs), 1)
    same = lax.rem(b, bs) // CAP == member_of(a)
    tok = jnp.where(same, token_of(a), rows)
    expert = lax.rem(outer + EXPERTS - lax.rem(b // bs, EXPERTS), EXPERTS)
    code = expert * CAP + lax.rem(b, CAP)
    mix = jnp.zeros((side, nc * bs), F32)
    for r, named, spot, gate in spots:
        mix = jnp.where((tok == r) & (code == named * CAP + spot), gate, mix)
    high = mix.astype(BF)
    gm[0] = high
    gm[1] = (mix - high.astype(F32)).astype(BF)

    scale = HEAD ** (-0.5)
    if x.shape[0] > n * CAP:
        x[n * CAP :, :] = jnp.zeros((x.shape[0] - n * CAP, x.shape[1]), BF)
    xl[...] = jnp.zeros(xl.shape, F32)
    iv[...] = jnp.zeros(iv.shape, F32)
    gs[...] = jnp.zeros(gs.shape, F32)
    loads[1].wait()
    loads[2].wait()
    wide = dq_ref[...].astype(F32)
    for c in range(KV):
        for m in range(MEM):
            i = c * MEM + m
            gain = gain_ref[:, i * HEAD : (i + 1) * HEAD]
            dqs[i : i + 1, :] = wide[:, i * HEAD : (i + 1) * HEAD]
            gs[m * tokens : (m + 1) * tokens, lanes[c]] = jnp.broadcast_to(gain, (tokens, HEAD))
            gs[mt + m : mt + m + 1, lanes[c]] = gain
    dq = dqs[...].astype(BF)
    dlen = dk_ref.shape[0]
    loads[3].wait()
    head_of = lax.broadcasted_iota(jnp.int32, (HEADS, dlen), 0) // MEM
    scores = jnp.zeros((HEADS, dlen), F32)
    for c in range(KV):
        part = lax.dot_general(
            dq, dk_ref[:, lanes[c]], (((1,), (1,)), ((), ())), preferred_element_type=F32
        )
        scores = jnp.where(head_of == c, part, scores)
    scores = scores * scale
    live = lax.broadcasted_iota(jnp.int32, (HEADS, dlen), 1) < len_ref[0]
    scores = jnp.where(live, scores, -1e30)
    peak = jnp.max(scores, axis=-1, keepdims=True)
    weights = jnp.where(live, jnp.exp(scores - peak), 0.0)
    total = jnp.sum(weights, axis=-1, keepdims=True)
    loads[4].wait()
    acc = jnp.zeros((HEADS, HEAD), F32)
    for c in range(KV):
        masked = jnp.where(head_of == c, weights, 0.0).astype(BF)
        acc = acc + jnp.dot(masked, dv_ref[:, lanes[c]], preferred_element_type=F32)
    dqs[...] = (acc / total).astype(BF).astype(F32)
    for c in range(KV):
        xl[mt : mt + MEM, lanes[c]] = dqs[c * MEM : (c + 1) * MEM, :]

    loads[5].wait()
    loads[6].wait()
    for copy in early:
        copy.wait_recv()
    returns = []
    count = EXPERTS * qrows
    a = lax.broadcasted_iota(jnp.int32, (HEAD, 2 * HEAD), 0)
    b = lax.broadcasted_iota(jnp.int32, (HEAD, 2 * HEAD), 1)
    spread = jnp.where(a == b // mt, 1.0, 0.0).astype(BF)
    a = lax.broadcasted_iota(jnp.int32, (count, 2 * HEAD), 0)
    b = lax.broadcasted_iota(jnp.int32, (count, 2 * HEAD), 1)
    sel = lax.rem(a, mt) == lax.rem(b, mt)
    lane = lax.broadcasted_iota(jnp.int32, (count, HEAD), 1)
    for j in range(hs):
        for i in range(j * EXPERTS * 2, (j + 1) * EXPERTS * 2):
            if i:
                sent[i].wait_recv()
        group = lax.rem(h + hs - j, hs)
        stats = jnp.zeros((count, HEAD), F32)
        first = pl.multiple_of(group * EXPERTS * 2, EXPERTS * 2)
        for c in range(HALF):
            sc = lax.dot_general(
                qg[c, qslot(group * EXPERTS, EXPERTS), :], k_ref[:, lanes[c]],
                (((1,), (1,)), ((), ())), preferred_element_type=F32,
            ) * scale
            pk = jnp.max(sc, axis=-1, keepdims=True).astype(BF).astype(F32)
            w = jnp.exp(sc - pk)
            tot = jnp.sum(w, axis=-1, keepdims=True)
            num = jnp.dot(w.astype(BF), v_ref[:, lanes[c]], preferred_element_type=F32)
            sb[pl.ds(first, EXPERTS * 2), c] = num.astype(BF).reshape(EXPERTS * 2, mt, HEAD)
            tot_high = tot.astype(BF).astype(F32)
            stats = jnp.where(lane == c, pk, stats)
            stats = jnp.where(lane == HALF + c, tot_high, stats)
            stats = jnp.where(lane == 2 * HALF + c, tot - tot_high, stats)
        compact = jnp.where(
            sel, jnp.dot(stats.astype(BF), spread, preferred_element_type=F32), 0.0
        )
        compact = jnp.sum(compact.reshape(EXPERTS * 2, mt, 2 * HEAD), axis=1)
        for i in range(EXPERTS * 2):
            st[first + i] = compact[i : i + 1]
        jj = (hs - j) % hs
        for d in sorted(range(EXPERTS), key=lambda d: -min(d, EXPERTS - d)):
            for rc in range(2):
                to = core if rc == 0 else other
                slot = slot_to(jj, d) * 2 + to
                i = (jj * EXPERTS + d) * 2 + rc
                pair = []
                for src, dst, ssem, rsem in (
                    (st.at[slot], rt.at[i], tsend.at[i], trecv.at[i]),
                    (sb.at[slot], rb.at[i], rsend.at[i], rrecv.at[i]),
                ):
                    if i == 0:
                        copy = pltpu.make_async_copy(src, dst, rsem)
                    else:
                        copy = remote(src, dst, ssem, rsem, there(jj, d, to))
                    copy.start()
                    pair.append(copy)
                returns.append((i, pair))
    returns.sort(key=lambda e: e[0])

    tr[...] = jnp.zeros(tr.shape, F32)
    low = lax.broadcasted_iota(jnp.int32, (nc, HEAD), 1) < HALF * mt
    scales = []
    for rc in range(2):
        found = list(range(rc, 2 * nc, 2))
        for i in found:
            copy = returns[i][1][0]
            copy.wait_recv() if i else copy.wait()
        stat = jnp.concatenate([rt[i] for i in found], axis=0)
        pk = stat[:, :HEAD]
        tot = pltpu.roll(pk, HALF * mt, 1) + stat[:, HEAD:]
        f = jnp.exp(jnp.minimum(pk - jnp.max(pk, axis=0, keepdims=True), 0.0))
        den = jnp.sum(jnp.where(low, f * tot, 1.0), axis=0, keepdims=True)
        tr[0:nc, :] = f / den
        scales.append(jnp.transpose(tr[...]))
    for rc in range(2):
        found = list(range(rc, 2 * nc, 2))
        source = core if rc == 0 else other
        for i in found:
            copy = returns[i][1][1]
            copy.wait_recv() if i else copy.wait()
        for c in range(HALF):
            acc = jnp.zeros((mt, HEAD), F32)
            for k, i in enumerate(found):
                acc = acc + rb[i, c].astype(F32) * scales[rc][c * mt : (c + 1) * mt, k : k + 1]
            xl[0:mt, pl.ds(pl.multiple_of(source * cols + c * HEAD, HEAD), HEAD)] = acc.astype(
                BF
            ).astype(F32)

    layer = xl[...]
    ss[...] = jnp.broadcast_to(
        jnp.sum(layer * layer, axis=1, keepdims=True) / (HEADS * HEAD), ss.shape
    )
    pre = ss[0:tokens, :]
    dec = ss[mt : mt + 1, :]
    for m in range(1, MEM):
        pre = pre + ss[m * tokens : (m + 1) * tokens, :]
        dec = dec + ss[mt + m : mt + m + 1, :]
    pre = lax.rsqrt(pre + 1e-05)
    for m in range(MEM):
        iv[m * tokens : (m + 1) * tokens, :] = pre
    iv[mt : mt + MEM, :] = jnp.broadcast_to(lax.rsqrt(dec + 1e-05), (MEM, HEAD))
    inv = iv[...]
    def xrow(slot, c):
        return pl.ds(pl.multiple_of((c * nc + slot) * bs, bs), bs)

    per = KV // PARTS
    moved = []
    for p in range(PARTS):
        block = lanes[p * per : (p + 1) * per]
        normed = jnp.concatenate([layer[:, s] * inv * gs[:, s] for s in block], axis=1).astype(BF)
        xs[p] = (
            jnp.dot(pm[...], normed, preferred_element_type=F32)
            .astype(BF)
            .reshape(EXPERTS, bs, per * HEAD)
        )
        out = {}
        for j, d in sorted(chips[1:], key=lambda jd: -(min(jd[1], EXPERTS - jd[1]) + (jd[0] > 0))):
            i = j * EXPERTS + d
            copy = remote(
                xs.at[p, lax.rem(outer + d, EXPERTS)], xg.at[p, xrow(mine, core)],
                gsend.at[p, i], grecv.at[p, i], there(j, d, core),
            )
            copy.start()
            out[j, d] = copy
        moved.append(out)
    shared = [[] for _ in range(PARTS)]
    for copy in early + list(sent.values()):
        copy.wait_send()
    for i, pair in returns:
        if i:
            for copy in pair:
                copy.wait_send()
    arrival = sorted(chips[1:], key=lambda jd: (min(jd[1], EXPERTS - jd[1]) + (jd[0] > 0)))

    def widen(p, where):
        for c in range(per):
            xf[p * per + c, where, :] = xg[p, where, lanes[c]].astype(F32)

    def first_half(p):
        where = xrow(mine, core)
        i = 2 + p * nc
        copy = remote(
            xs.at[p, outer], xg.at[p, where], psend.at[i], precv.at[i], partner
        )
        copy.start()
        shared[p].append(copy)
        xg[p, where, :] = xs[p, outer]
        widen(p, where)
        for j, d in arrival:
            moved[p][j, d].wait_recv()
            where = xrow(slot_from(j, d), core)
            i = 2 + p * nc + j * EXPERTS + d
            copy = remote(xg.at[p, where], xg.at[p, where], psend.at[i], precv.at[i], partner)
            copy.start()
            shared[p].append(copy)
            widen(p, where)

    def second_half(p):
        for copy, (j, d) in zip(shared[p], [(0, 0)] + arrival):
            copy.wait_recv()
            widen(p, xrow(slot_from(j, d), other))
        for k in range(CAP):
            for c in range(p * per, (p + 1) * per):
                for m in range(MEM):
                    i = c * MEM + m
                    x[k * n : (k + 1) * n, i * HEAD : (i + 1) * HEAD] = xf[
                        c, pl.ds(m * CAP + k, n, stride=bs), :
                    ].astype(BF)

    ff = wg_ref.shape[1]
    step = 256 if ff % 256 == 0 else ff
    steps = ff // step
    deep = per * MEM * HEAD

    def up(p, i):
        where = slice(i * step, (i + 1) * step)
        part = slice(p * deep, (p + 1) * deep)
        gated = jnp.dot(x[:, part], wg_ref[part, where], preferred_element_type=F32)
        raised = jnp.dot(x[:, part], wu_ref[part, where], preferred_element_type=F32)
        if p:
            gated = gated + ga[:, where]
            raised = raised + ua[:, where]
        if p < PARTS - 1:
            ga[:, where] = gated
            ua[:, where] = raised
        else:
            hid[:, where] = (gated / (1.0 + jnp.exp(-gated)) * raised).astype(BF)

    first_half(0)
    second_half(0)
    for load in loads[7:9]:
        load.wait()
    for p in range(PARTS):
        middle = (steps * 4) // 7 if p < PARTS - 1 else steps
        for i in range(middle):
            up(p, i)
        if p < PARTS - 1:
            first_half(p + 1)
            for i in range(middle, steps):
                up(p, i)
            second_half(p + 1)
    loads[9].wait()

    each = KV // CHUNKS
    width = each * HEAD
    far = nc * bs
    swaps = []
    outs = []

    def down(g):
        for e in range(each):
            c = g * each + e
            piece = jnp.dot(
                hid[...], wd_ref[:, c * MEM * HEAD : (c + 1) * MEM * HEAD], preferred_element_type=F32
            )[: n * CAP].astype(BF).astype(F32)
            for k in range(CAP):
                for m in range(MEM):
                    pf[c, pl.ds(m * CAP + k, n, stride=bs), :] = piece[k * n : (k + 1) * n, lanes[m]]
            pb[g, :, lanes[e]] = pf[c, pl.ds(pl.multiple_of(other * far, far), far), :].astype(BF)
        i = 2 + PARTS * nc + g
        copy = remote(pb.at[g], p1.at[g], psend.at[i], precv.at[i], partner)
        copy.start()
        swaps.append(copy)

    def send_out(g, near):
        for o in range(EXPERTS):
            for hh in range(hs):
                if (o + hh == 0) != near:
                    continue
                d = lax.rem(o + EXPERTS - outer, EXPERTS)
                j = lax.rem(hh + hs - h, hs)
                i = j * EXPERTS + d

                @pl.when(i != 0)
                def _(o=o, hh=hh, i=i, g=g):
                    remote(
                        ys.at[g, pl.ds((hh * EXPERTS + o) * bs, bs)],
                        yr.at[g, pl.ds(pl.multiple_of(i * bs, bs), bs)],
                        ysend.at[g, i], yrecv.at[g, i], at(o, hh, core),
                    ).start()

    def deliver(g):
        swaps[g].wait_recv()
        for e in range(each):
            c = g * each + e
            ys[g, :, lanes[e]] = (
                pf[c, pl.ds(pl.multiple_of(core * far, far), far), :]
                + p1[g, :, lanes[e]].astype(F32)
            ).astype(BF)
        for i in range(1, nc):
            outs.append(
                remote(
                    ys.at[g, pl.ds(i * bs, bs)], yr.at[g, pl.ds(i * bs, bs)],
                    ysend.at[g, i], yrecv.at[g, i], partner,
                )
            )
        send_out(g, True)
        if g == CHUNKS - 1:
            for late in range(1, CHUNKS):
                send_out(late, False)
        if g == 0:
            send_out(g, False)
        yr[g, 0:bs, :] = ys[g, pl.ds(pl.multiple_of(mine * bs, bs), bs), :]

    for g in range(CHUNKS + 2):
        if g < CHUNKS:
            down(g)
        if g >= 2:
            deliver(g - 2)
    each_out = nc - 1
    for copy in swaps:
        copy.wait_send()
    for p in range(PARTS):
        for copy in list(moved[p].values()) + shared[p]:
            copy.wait_send()
    for g in range(CHUNKS):
        for copy in outs[g * each_out : (g + 1) * each_out]:
            copy.wait_recv()
        where = slice(g * width, (g + 1) * width)
        osc[:, where] = (
            xl[:, where]
            + jnp.dot(gm[0], yr[g], preferred_element_type=F32)
            + jnp.dot(gm[1], yr[g], preferred_element_type=F32)
        )
        for c in range(g * each, (g + 1) * each):
            for m in range(MEM):
                i = c * MEM + m
                out_ref[0:tokens, i * HEAD : (i + 1) * HEAD] = osc[
                    m * tokens : (m + 1) * tokens, lanes[c]
                ].astype(BF)
                out_ref[tokens:rows, i * HEAD : (i + 1) * HEAD] = osc[
                    mt + m : mt + m + 1, lanes[c]
                ].astype(BF)
        for copy in outs[g * each_out : (g + 1) * each_out]:
            copy.wait_send()


def on_device(n, *args):
    (q, k, v, dq, dk, dv, dlen, idx, gate, gain, wg, wu, wd) = args
    width = q.shape[1]
    tokens = q.shape[0]
    rows = tokens + dq.shape[0]
    nc = n // 2
    ff = wg.shape[2]
    mt, bs = MEM * tokens, MEM * CAP
    side = (mt + MEM + 15) // 16 * 16
    wide = max(n * CAP, FULL)
    lanes = KV * HEAD
    hbm = pl.BlockSpec(memory_space=pl.ANY)
    vm = pl.BlockSpec(memory_space=pltpu.VMEM)
    positions = 2 * k.shape[0]
    dma = pltpu.SemaphoreType.DMA
    out = pl.pallas_call(
        functools.partial(body, n),
        out_shape=pltpu.VMEM((rows, width), BF),
        in_specs=[hbm] * 13,
        out_specs=vm,
        scratch_shapes=[
            pltpu.SMEM(dlen.shape, jnp.int32),
            pltpu.SMEM(idx.T.shape, jnp.int32),
            pltpu.SMEM(gate.T.shape, F32),
            pltpu.VMEM(q.shape, BF),
            pltpu.VMEM(dq.shape, BF),
            pltpu.VMEM((1, width), F32),
            pltpu.VMEM((positions, HALF * HEAD), BF),
            pltpu.VMEM((positions, HALF * HEAD), BF),
            pltpu.VMEM(dk.shape[1:], BF),
            pltpu.VMEM(dv.shape[1:], BF),
            pltpu.VMEM(wg.shape[1:], BF),
            pltpu.VMEM(wu.shape[1:], BF),
            pltpu.VMEM(wd.shape[1:], BF),
            pltpu.VMEM((KV, mt, HEAD), F32),
            pltpu.VMEM((2, HALF, mt, HEAD), BF),
            pltpu.VMEM((HALF, nc * 2 * mt, HEAD), BF),
            pltpu.VMEM((n, HALF, mt, HEAD), BF),
            pltpu.VMEM((n, HALF, mt, HEAD), BF),
            pltpu.VMEM((n, 1, 2 * HEAD), F32),
            pltpu.VMEM((n, 1, 2 * HEAD), F32),
            pltpu.VMEM((HEAD, HEAD), F32),
            pltpu.VMEM((HEADS, HEAD), F32),
            pltpu.VMEM((side, lanes), F32),
            pltpu.VMEM((side, lanes), F32),
            pltpu.VMEM((side, HEAD), F32),
            pltpu.VMEM((side, HEAD), F32),
            pltpu.VMEM((EXPERTS * bs, side), BF),
            pltpu.VMEM((2, side, nc * bs), BF),
            pltpu.VMEM((PARTS, EXPERTS, bs, lanes // PARTS), BF),
            pltpu.VMEM((PARTS, n * bs, lanes // PARTS), BF),
            pltpu.VMEM((KV, n * bs, HEAD), F32),
            pltpu.VMEM((wide, width), BF),
            pltpu.VMEM((wide, ff), F32),
            pltpu.VMEM((wide, ff), F32),
            pltpu.VMEM((wide, ff), BF),
            pltpu.VMEM((KV, n * bs, HEAD), F32),
            pltpu.VMEM((CHUNKS, nc * bs, lanes // CHUNKS), BF),
            pltpu.VMEM((CHUNKS, nc * bs, lanes // CHUNKS), BF),
            pltpu.VMEM((CHUNKS, nc * bs, lanes // CHUNKS), BF),
            pltpu.VMEM((CHUNKS, nc * bs, lanes // CHUNKS), BF),
            pltpu.VMEM((side, lanes), F32),
            dma((n,)),
            dma((n,)),
            dma((PARTS, nc)),
            dma((PARTS, nc)),
            dma((n,)),
            dma((n,)),
            dma((n,)),
            dma((n,)),
            dma((2 + PARTS * nc + CHUNKS,)),
            dma((2 + PARTS * nc + CHUNKS,)),
            dma((CHUNKS, nc)),
            dma((CHUNKS, nc)),
            dma((13,)),
        ],
        compiler_params=pltpu.CompilerParams(
            collective_id=0, has_side_effects=True, vmem_limit_bytes=60_000_000
        ),
        name="moe_layer",
    )(q, dq, dlen, idx.T, gate.T, gain[None], k, v, dk, dv, wg, wu, wd)
    return out[:tokens], out[tokens:]


def solution(mesh):
    both = ("groups", "seq")
    in_specs = (
        P(both, None),
        P(both, None),
        P(both, None),
        P(both, None),
        P(both, None, None),
        P(both, None, None),
        P(both),
        P(both, None),
        P(both, None),
        P(),
        P("seq", None, None),
        P("seq", None, None),
        P("seq", None, None),
    )
    return jax.shard_map(
        functools.partial(on_device, mesh.shape["seq"]),
        mesh=mesh,
        in_specs=in_specs,
        out_specs=(P(both, None), P(both, None)),
        check_vma=False,
    )
```

```python
import functools

import jax
import jax.numpy as jnp
from jax import lax
from jax.experimental import pallas as pl
from jax.experimental.pallas import tpu as pltpu
from jax.sharding import PartitionSpec as P

HEADS = 32
KV = 8
MEM = HEADS // KV
HEAD = 128
EXPERTS = 4
CAP = 4
HALF = KV // 2
F32 = jnp.float32
BF = jnp.bfloat16
CHUNKS = 4
FULL = 128
PARTS = 2
MESH = pl.DeviceIdType.MESH


def body(
    n,
    q_hbm,
    dq_hbm,
    len_hbm,
    idx_hbm,
    gate_hbm,
    gain_hbm,
    k_hbm,
    v_hbm,
    dk_hbm,
    dv_hbm,
    wg_hbm,
    wu_hbm,
    wd_hbm,
    out_ref,
    len_ref,
    idx_ref,
    gate_ref,
    q_ref,
    dq_ref,
    gain_ref,
    k_ref,
    v_ref,
    dk_ref,
    dv_ref,
    wg_ref,
    wu_ref,
    wd_ref,
    qs,
    qh,
    qg,
    sb,
    rb,
    st,
    rt,
    tr,
    dqs,
    gs,
    xl,
    ss,
    iv,
    pm,
    gm,
    xs,
    xg,
    xf,
    x,
    ga,
    ua,
    hid,
    pf,
    pb,
    p1,
    ys,
    yr,
    osc,
    qsend,
    qrecv,
    gsend,
    grecv,
    rsend,
    rrecv,
    tsend,
    trecv,
    psend,
    precv,
    ysend,
    yrecv,
    local,
):
    hs = n // (2 * EXPERTS)
    nc = hs * EXPERTS
    me = lax.axis_index("seq")
    core = lax.rem(me, 2)
    h = lax.rem(me // 2, hs)
    outer = me // (2 * hs)
    other = 1 - core

    def at(o, hh, c):
        return {"seq": (o * hs + hh) * 2 + c}

    def there(j, d, c):
        return at(lax.rem(outer + d, EXPERTS), lax.rem(h + j, hs), c)

    def slot_to(j, d):
        return lax.rem(h + j, hs) * EXPERTS + lax.rem(outer + d, EXPERTS)

    def slot_from(j, d):
        return lax.rem(h + hs - j, hs) * EXPERTS + lax.rem(outer + EXPERTS - d, EXPERTS)

    partner = at(outer, h, other)
    mine = h * EXPERTS + outer
    chips = [(j, d) for j in range(hs) for d in range(EXPERTS)]
    barrier = pltpu.get_barrier_semaphore()
    for j, d in chips:
        for c in (core, other):
            if (j, d) != (0, 0) or c is other:
                pl.semaphore_signal(barrier, inc=1, device_id=there(j, d, c), device_id_type=MESH)

    length = k_ref.shape[0] // 2
    cols = HALF * HEAD

    def half(c):
        return pl.ds(pl.multiple_of(c * cols, cols), cols)

    sources = [
        (q_hbm, q_ref),
        (dq_hbm, dq_ref),
        (gain_hbm, gain_ref),
        (dk_hbm.at[0], dk_ref),
        (dv_hbm.at[0], dv_ref),
        (k_hbm.at[:, half(core)], k_ref.at[pl.ds(0, length)]),
        (v_hbm.at[:, half(core)], v_ref.at[pl.ds(0, length)]),
        (wg_hbm.at[0], wg_ref),
        (wu_hbm.at[0], wu_ref),
        (wd_hbm.at[0], wd_ref),
        (len_hbm, len_ref),
        (idx_hbm, idx_ref),
        (gate_hbm, gate_ref),
    ]
    loads = [pltpu.make_async_copy(s, t, local.at[i]) for i, (s, t) in enumerate(sources)]
    for load in loads[:3] + loads[10:] + loads[3:7]:
        load.start()

    def remote(src, dst, ssem, rsem, peer):
        return pltpu.make_async_remote_copy(
            src_ref=src, dst_ref=dst, send_sem=ssem, recv_sem=rsem,
            device_id=peer, device_id_type=MESH,
        )

    tokens = q_ref.shape[0]
    rows = tokens + 1
    mt = MEM * tokens
    bs = MEM * CAP
    lanes = [slice(c * HEAD, (c + 1) * HEAD) for c in range(KV)]

    loads[0].wait()
    wide = q_ref[...].astype(F32)
    for c in range(KV):
        for m in range(MEM):
            i = c * MEM + m
            qs[c, m * tokens : (m + 1) * tokens, :] = wide[:, i * HEAD : (i + 1) * HEAD]
    for c in range(2):
        qh[c] = qs[c * HALF : (c + 1) * HALF].astype(BF)

    pl.semaphore_wait(barrier, n - 1)
    early = [
        remote(k_hbm.at[:, half(other)], k_ref.at[pl.ds(length, length)], psend.at[0], precv.at[0], partner),
        remote(v_hbm.at[:, half(other)], v_ref.at[pl.ds(length, length)], psend.at[1], precv.at[1], partner),
    ]
    here = mine * 2 + core
    sent = {}
    for j, d in chips:
        for rc in range(2):
            to = core if rc == 0 else other
            i = (j * EXPERTS + d) * 2 + rc
            if i:
                copy = remote(
                    qh.at[to], qg.at[here], qsend.at[i], qrecv.at[i], there(j, d, to)
                )
                copy.start()
                sent[i] = copy
    qg[here] = qh[core]
    for copy in early:
        copy.start()
    for load in loads[7:10]:
        load.start()
    for load in loads[10:]:
        load.wait()

    spots = []
    for r in range(rows):
        for t in range(idx_ref.shape[0]):
            named = idx_ref[t, r]
            spot = jnp.int32(0)
            for before in range(r):
                hit = (idx_ref[0, before] == named) | (idx_ref[1, before] == named)
                spot = spot + jnp.where(hit, 1, 0)
            spots.append((r, named, spot, gate_ref[t, r]))

    def token_of(i):
        return jnp.where(i < mt, lax.rem(i, tokens), jnp.where(i < mt + MEM, tokens, rows))

    def member_of(i):
        return jnp.where(i < mt, i // tokens, i - mt)

    side = xl.shape[0]
    a = lax.broadcasted_iota(jnp.int32, (EXPERTS * bs, side), 0)
    b = lax.broadcasted_iota(jnp.int32, (EXPERTS * bs, side), 1)
    same = lax.rem(a, bs) // CAP == member_of(b)
    pick = jnp.zeros((EXPERTS * bs, side), F32)
    code = a // bs * CAP + lax.rem(a, CAP)
    tok = jnp.where(same, token_of(b), rows)
    for r, named, spot, _ in spots:
        pick = jnp.where((tok == r) & (code == named * CAP + spot), 1.0, pick)
    pm[...] = pick.astype(BF)
    a = lax.broadcasted_iota(jnp.int32, (side, nc * bs), 0)
    b = lax.broadcasted_iota(jnp.int32, (side, nc * bs), 1)
    same = lax.rem(b, bs) // CAP == member_of(a)
    tok = jnp.where(same, token_of(a), rows)
    expert = lax.rem(outer + EXPERTS - lax.rem(b // bs, EXPERTS), EXPERTS)
    code = expert * CAP + lax.rem(b, CAP)
    mix = jnp.zeros((side, nc * bs), F32)
    for r, named, spot, gate in spots:
        mix = jnp.where((tok == r) & (code == named * CAP + spot), gate, mix)
    high = mix.astype(BF)
    gm[0] = high
    gm[1] = (mix - high.astype(F32)).astype(BF)

    scale = HEAD ** (-0.5)
    if x.shape[0] > n * CAP:
        x[n * CAP :, :] = jnp.zeros((x.shape[0] - n * CAP, x.shape[1]), BF)
    xl[...] = jnp.zeros(xl.shape, F32)
    iv[...] = jnp.zeros(iv.shape, F32)
    gs[...] = jnp.zeros(gs.shape, F32)
    loads[1].wait()
    loads[2].wait()
    wide = dq_ref[...].astype(F32)
    for c in range(KV):
        for m in range(MEM):
            i = c * MEM + m
            gain = gain_ref[:, i * HEAD : (i + 1) * HEAD]
            dqs[i : i + 1, :] = wide[:, i * HEAD : (i + 1) * HEAD]
            gs[m * tokens : (m + 1) * tokens, lanes[c]] = jnp.broadcast_to(gain, (tokens, HEAD))
            gs[mt + m : mt + m + 1, lanes[c]] = gain
    dq = dqs[...].astype(BF)
    dlen = dk_ref.shape[0]
    loads[3].wait()
    head_of = lax.broadcasted_iota(jnp.int32, (HEADS, dlen), 0) // MEM
    scores = jnp.zeros((HEADS, dlen), F32)
    for c in range(KV):
        part = lax.dot_general(
            dq, dk_ref[:, lanes[c]], (((1,), (1,)), ((), ())), preferred_element_type=F32
        )
        scores = jnp.where(head_of == c, part, scores)
    scores = scores * scale
    live = lax.broadcasted_iota(jnp.int32, (HEADS, dlen), 1) < len_ref[0]
    scores = jnp.where(live, scores, -1e30)
    peak = jnp.max(scores, axis=-1, keepdims=True)
    weights = jnp.where(live, jnp.exp(scores - peak), 0.0)
    total = jnp.sum(weights, axis=-1, keepdims=True)
    loads[4].wait()
    acc = jnp.zeros((HEADS, HEAD), F32)
    for c in range(KV):
        masked = jnp.where(head_of == c, weights, 0.0).astype(BF)
        acc = acc + jnp.dot(masked, dv_ref[:, lanes[c]], preferred_element_type=F32)
    dqs[...] = (acc / total).astype(BF).astype(F32)
    for c in range(KV):
        xl[mt : mt + MEM, lanes[c]] = dqs[c * MEM : (c + 1) * MEM, :]

    loads[5].wait()
    loads[6].wait()
    for copy in early:
        copy.wait_recv()
    returns = []
    count = EXPERTS * 2 * mt
    a = lax.broadcasted_iota(jnp.int32, (HEAD, 2 * HEAD), 0)
    b = lax.broadcasted_iota(jnp.int32, (HEAD, 2 * HEAD), 1)
    spread = jnp.where(a == b // mt, 1.0, 0.0).astype(BF)
    a = lax.broadcasted_iota(jnp.int32, (count, 2 * HEAD), 0)
    b = lax.broadcasted_iota(jnp.int32, (count, 2 * HEAD), 1)
    sel = lax.rem(a, mt) == lax.rem(b, mt)
    lane = lax.broadcasted_iota(jnp.int32, (count, HEAD), 1)
    for j in range(hs):
        for i in range(j * EXPERTS * 2, (j + 1) * EXPERTS * 2):
            if i:
                sent[i].wait_recv()
        group = lax.rem(h + hs - j, hs)
        stats = jnp.zeros((count, HEAD), F32)
        first = pl.multiple_of(group * EXPERTS * 2, EXPERTS * 2)
        for c in range(HALF):
            sc = lax.dot_general(
                qg[pl.ds(first, EXPERTS * 2), c].reshape(count, HEAD), k_ref[:, lanes[c]],
                (((1,), (1,)), ((), ())), preferred_element_type=F32,
            ) * scale
            pk = jnp.max(sc, axis=-1, keepdims=True).astype(BF).astype(F32)
            w = jnp.exp(sc - pk)
            tot = jnp.sum(w, axis=-1, keepdims=True)
            num = jnp.dot(w.astype(BF), v_ref[:, lanes[c]], preferred_element_type=F32)
            sb[pl.ds(first, EXPERTS * 2), c] = num.astype(BF).reshape(EXPERTS * 2, mt, HEAD)
            tot_high = tot.astype(BF).astype(F32)
            stats = jnp.where(lane == c, pk, stats)
            stats = jnp.where(lane == HALF + c, tot_high, stats)
            stats = jnp.where(lane == 2 * HALF + c, tot - tot_high, stats)
        compact = jnp.where(
            sel, jnp.dot(stats.astype(BF), spread, preferred_element_type=F32), 0.0
        )
        compact = jnp.sum(compact.reshape(EXPERTS * 2, mt, 2 * HEAD), axis=1)
        for i in range(EXPERTS * 2):
            st[first + i] = compact[i : i + 1]
        jj = (hs - j) % hs
        for d in sorted(range(EXPERTS), key=lambda d: -min(d, EXPERTS - d)):
            for rc in range(2):
                to = core if rc == 0 else other
                slot = slot_to(jj, d) * 2 + to
                i = (jj * EXPERTS + d) * 2 + rc
                pair = []
                for src, dst, ssem, rsem in (
                    (st.at[slot], rt.at[i], tsend.at[i], trecv.at[i]),
                    (sb.at[slot], rb.at[i], rsend.at[i], rrecv.at[i]),
                ):
                    if i == 0:
                        copy = pltpu.make_async_copy(src, dst, rsem)
                    else:
                        copy = remote(src, dst, ssem, rsem, there(jj, d, to))
                    copy.start()
                    pair.append(copy)
                returns.append((i, pair))
    returns.sort(key=lambda e: e[0])

    tr[...] = jnp.zeros(tr.shape, F32)
    low = lax.broadcasted_iota(jnp.int32, (nc, HEAD), 1) < HALF * mt
    scales = []
    for rc in range(2):
        found = list(range(rc, 2 * nc, 2))
        for i in found:
            copy = returns[i][1][0]
            copy.wait_recv() if i else copy.wait()
        stat = jnp.concatenate([rt[i] for i in found], axis=0)
        pk = stat[:, :HEAD]
        tot = pltpu.roll(pk, HALF * mt, 1) + stat[:, HEAD:]
        f = jnp.exp(jnp.minimum(pk - jnp.max(pk, axis=0, keepdims=True), 0.0))
        den = jnp.sum(jnp.where(low, f * tot, 1.0), axis=0, keepdims=True)
        tr[0:nc, :] = f / den
        scales.append(jnp.transpose(tr[...]))
    for rc in range(2):
        found = list(range(rc, 2 * nc, 2))
        source = core if rc == 0 else other
        for i in found:
            copy = returns[i][1][1]
            copy.wait_recv() if i else copy.wait()
        for c in range(HALF):
            acc = jnp.zeros((mt, HEAD), F32)
            for k, i in enumerate(found):
                acc = acc + rb[i, c].astype(F32) * scales[rc][c * mt : (c + 1) * mt, k : k + 1]
            xl[0:mt, pl.ds(pl.multiple_of(source * cols + c * HEAD, HEAD), HEAD)] = acc.astype(
                BF
            ).astype(F32)

    layer = xl[...]
    ss[...] = jnp.broadcast_to(
        jnp.sum(layer * layer, axis=1, keepdims=True) / (HEADS * HEAD), ss.shape
    )
    pre = ss[0:tokens, :]
    dec = ss[mt : mt + 1, :]
    for m in range(1, MEM):
        pre = pre + ss[m * tokens : (m + 1) * tokens, :]
        dec = dec + ss[mt + m : mt + m + 1, :]
    pre = lax.rsqrt(pre + 1e-05)
    for m in range(MEM):
        iv[m * tokens : (m + 1) * tokens, :] = pre
    iv[mt : mt + MEM, :] = jnp.broadcast_to(lax.rsqrt(dec + 1e-05), (MEM, HEAD))
    inv = iv[...]
    def xrow(slot, c):
        return pl.ds(pl.multiple_of((c * nc + slot) * bs, bs), bs)

    per = KV // PARTS
    moved = []
    for p in range(PARTS):
        block = lanes[p * per : (p + 1) * per]
        normed = jnp.concatenate([layer[:, s] * inv * gs[:, s] for s in block], axis=1).astype(BF)
        xs[p] = (
            jnp.dot(pm[...], normed, preferred_element_type=F32)
            .astype(BF)
            .reshape(EXPERTS, bs, per * HEAD)
        )
        out = {}
        for j, d in sorted(chips[1:], key=lambda jd: -(min(jd[1], EXPERTS - jd[1]) + (jd[0] > 0))):
            i = j * EXPERTS + d
            copy = remote(
                xs.at[p, lax.rem(outer + d, EXPERTS)], xg.at[p, xrow(mine, core)],
                gsend.at[p, i], grecv.at[p, i], there(j, d, core),
            )
            copy.start()
            out[j, d] = copy
        moved.append(out)
    shared = [[] for _ in range(PARTS)]
    for copy in early + list(sent.values()):
        copy.wait_send()
    for i, pair in returns:
        if i:
            for copy in pair:
                copy.wait_send()
    arrival = sorted(chips[1:], key=lambda jd: (min(jd[1], EXPERTS - jd[1]) + (jd[0] > 0)))

    def widen(p, where):
        for c in range(per):
            xf[p * per + c, where, :] = xg[p, where, lanes[c]].astype(F32)

    def first_half(p):
        where = xrow(mine, core)
        i = 2 + p * nc
        copy = remote(
            xs.at[p, outer], xg.at[p, where], psend.at[i], precv.at[i], partner
        )
        copy.start()
        shared[p].append(copy)
        xg[p, where, :] = xs[p, outer]
        widen(p, where)
        for j, d in arrival:
            moved[p][j, d].wait_recv()
            where = xrow(slot_from(j, d), core)
            i = 2 + p * nc + j * EXPERTS + d
            copy = remote(xg.at[p, where], xg.at[p, where], psend.at[i], precv.at[i], partner)
            copy.start()
            shared[p].append(copy)
            widen(p, where)

    def second_half(p):
        for copy, (j, d) in zip(shared[p], [(0, 0)] + arrival):
            copy.wait_recv()
            widen(p, xrow(slot_from(j, d), other))
        for k in range(CAP):
            for c in range(p * per, (p + 1) * per):
                for m in range(MEM):
                    i = c * MEM + m
                    x[k * n : (k + 1) * n, i * HEAD : (i + 1) * HEAD] = xf[
                        c, pl.ds(m * CAP + k, n, stride=bs), :
                    ].astype(BF)

    ff = wg_ref.shape[1]
    step = 256 if ff % 256 == 0 else ff
    steps = ff // step
    deep = per * MEM * HEAD

    def up(p, i):
        where = slice(i * step, (i + 1) * step)
        part = slice(p * deep, (p + 1) * deep)
        gated = jnp.dot(x[:, part], wg_ref[part, where], preferred_element_type=F32)
        raised = jnp.dot(x[:, part], wu_ref[part, where], preferred_element_type=F32)
        if p:
            gated = gated + ga[:, where]
            raised = raised + ua[:, where]
        if p < PARTS - 1:
            ga[:, where] = gated
            ua[:, where] = raised
        else:
            hid[:, where] = (gated / (1.0 + jnp.exp(-gated)) * raised).astype(BF)

    first_half(0)
    second_half(0)
    for load in loads[7:9]:
        load.wait()
    for p in range(PARTS):
        middle = (steps * 4) // 7 if p < PARTS - 1 else steps
        for i in range(middle):
            up(p, i)
        if p < PARTS - 1:
            first_half(p + 1)
            for i in range(middle, steps):
                up(p, i)
            second_half(p + 1)
    loads[9].wait()

    each = KV // CHUNKS
    width = each * HEAD
    far = nc * bs
    swaps = []
    outs = []

    def down(g):
        for e in range(each):
            c = g * each + e
            piece = jnp.dot(
                hid[...], wd_ref[:, c * MEM * HEAD : (c + 1) * MEM * HEAD], preferred_element_type=F32
            )[: n * CAP].astype(BF).astype(F32)
            for k in range(CAP):
                for m in range(MEM):
                    pf[c, pl.ds(m * CAP + k, n, stride=bs), :] = piece[k * n : (k + 1) * n, lanes[m]]
            pb[g, :, lanes[e]] = pf[c, pl.ds(pl.multiple_of(other * far, far), far), :].astype(BF)
        i = 2 + PARTS * nc + g
        copy = remote(pb.at[g], p1.at[g], psend.at[i], precv.at[i], partner)
        copy.start()
        swaps.append(copy)

    def send_out(g, near):
        for o in range(EXPERTS):
            for hh in range(hs):
                if (o + hh == 0) != near:
                    continue
                d = lax.rem(o + EXPERTS - outer, EXPERTS)
                j = lax.rem(hh + hs - h, hs)
                i = j * EXPERTS + d

                @pl.when(i != 0)
                def _(o=o, hh=hh, i=i, g=g):
                    remote(
                        ys.at[g, pl.ds((hh * EXPERTS + o) * bs, bs)],
                        yr.at[g, pl.ds(pl.multiple_of(i * bs, bs), bs)],
                        ysend.at[g, i], yrecv.at[g, i], at(o, hh, core),
                    ).start()

    def deliver(g):
        swaps[g].wait_recv()
        for e in range(each):
            c = g * each + e
            ys[g, :, lanes[e]] = (
                pf[c, pl.ds(pl.multiple_of(core * far, far), far), :]
                + p1[g, :, lanes[e]].astype(F32)
            ).astype(BF)
        for i in range(1, nc):
            outs.append(
                remote(
                    ys.at[g, pl.ds(i * bs, bs)], yr.at[g, pl.ds(i * bs, bs)],
                    ysend.at[g, i], yrecv.at[g, i], partner,
                )
            )
        send_out(g, True)
        if g == CHUNKS - 1:
            for late in range(1, CHUNKS):
                send_out(late, False)
        if g == 0:
            send_out(g, False)
        yr[g, 0:bs, :] = ys[g, pl.ds(pl.multiple_of(mine * bs, bs), bs), :]

    for g in range(CHUNKS + 2):
        if g < CHUNKS:
            down(g)
        if g >= 2:
            deliver(g - 2)
    each_out = nc - 1
    for copy in swaps:
        copy.wait_send()
    for p in range(PARTS):
        for copy in list(moved[p].values()) + shared[p]:
            copy.wait_send()
    for g in range(CHUNKS):
        for copy in outs[g * each_out : (g + 1) * each_out]:
            copy.wait_recv()
        where = slice(g * width, (g + 1) * width)
        osc[:, where] = (
            xl[:, where]
            + jnp.dot(gm[0], yr[g], preferred_element_type=F32)
            + jnp.dot(gm[1], yr[g], preferred_element_type=F32)
        )
        for c in range(g * each, (g + 1) * each):
            for m in range(MEM):
                i = c * MEM + m
                out_ref[0:tokens, i * HEAD : (i + 1) * HEAD] = osc[
                    m * tokens : (m + 1) * tokens, lanes[c]
                ].astype(BF)
                out_ref[tokens:rows, i * HEAD : (i + 1) * HEAD] = osc[
                    mt + m : mt + m + 1, lanes[c]
                ].astype(BF)
        for copy in outs[g * each_out : (g + 1) * each_out]:
            copy.wait_send()


def on_device(n, *args):
    (q, k, v, dq, dk, dv, dlen, idx, gate, gain, wg, wu, wd) = args
    width = q.shape[1]
    tokens = q.shape[0]
    rows = tokens + dq.shape[0]
    nc = n // 2
    ff = wg.shape[2]
    mt, bs = MEM * tokens, MEM * CAP
    side = (mt + MEM + 15) // 16 * 16
    wide = max(n * CAP, FULL)
    lanes = KV * HEAD
    hbm = pl.BlockSpec(memory_space=pl.ANY)
    vm = pl.BlockSpec(memory_space=pltpu.VMEM)
    positions = 2 * k.shape[0]
    dma = pltpu.SemaphoreType.DMA
    out = pl.pallas_call(
        functools.partial(body, n),
        out_shape=pltpu.VMEM((rows, width), BF),
        in_specs=[hbm] * 13,
        out_specs=vm,
        scratch_shapes=[
            pltpu.SMEM(dlen.shape, jnp.int32),
            pltpu.SMEM(idx.T.shape, jnp.int32),
            pltpu.SMEM(gate.T.shape, F32),
            pltpu.VMEM(q.shape, BF),
            pltpu.VMEM(dq.shape, BF),
            pltpu.VMEM((1, width), F32),
            pltpu.VMEM((positions, HALF * HEAD), BF),
            pltpu.VMEM((positions, HALF * HEAD), BF),
            pltpu.VMEM(dk.shape[1:], BF),
            pltpu.VMEM(dv.shape[1:], BF),
            pltpu.VMEM(wg.shape[1:], BF),
            pltpu.VMEM(wu.shape[1:], BF),
            pltpu.VMEM(wd.shape[1:], BF),
            pltpu.VMEM((KV, mt, HEAD), F32),
            pltpu.VMEM((2, HALF, mt, HEAD), BF),
            pltpu.VMEM((n, HALF, mt, HEAD), BF),
            pltpu.VMEM((n, HALF, mt, HEAD), BF),
            pltpu.VMEM((n, HALF, mt, HEAD), BF),
            pltpu.VMEM((n, 1, 2 * HEAD), F32),
            pltpu.VMEM((n, 1, 2 * HEAD), F32),
            pltpu.VMEM((HEAD, HEAD), F32),
            pltpu.VMEM((HEADS, HEAD), F32),
            pltpu.VMEM((side, lanes), F32),
            pltpu.VMEM((side, lanes), F32),
            pltpu.VMEM((side, HEAD), F32),
            pltpu.VMEM((side, HEAD), F32),
            pltpu.VMEM((EXPERTS * bs, side), BF),
            pltpu.VMEM((2, side, nc * bs), BF),
            pltpu.VMEM((PARTS, EXPERTS, bs, lanes // PARTS), BF),
            pltpu.VMEM((PARTS, n * bs, lanes // PARTS), BF),
            pltpu.VMEM((KV, n * bs, HEAD), F32),
            pltpu.VMEM((wide, width), BF),
            pltpu.VMEM((wide, ff), F32),
            pltpu.VMEM((wide, ff), F32),
            pltpu.VMEM((wide, ff), BF),
            pltpu.VMEM((KV, n * bs, HEAD), F32),
            pltpu.VMEM((CHUNKS, nc * bs, lanes // CHUNKS), BF),
            pltpu.VMEM((CHUNKS, nc * bs, lanes // CHUNKS), BF),
            pltpu.VMEM((CHUNKS, nc * bs, lanes // CHUNKS), BF),
            pltpu.VMEM((CHUNKS, nc * bs, lanes // CHUNKS), BF),
            pltpu.VMEM((side, lanes), F32),
            dma((n,)),
            dma((n,)),
            dma((PARTS, nc)),
            dma((PARTS, nc)),
            dma((n,)),
            dma((n,)),
            dma((n,)),
            dma((n,)),
            dma((2 + PARTS * nc + CHUNKS,)),
            dma((2 + PARTS * nc + CHUNKS,)),
            dma((CHUNKS, nc)),
            dma((CHUNKS, nc)),
            dma((13,)),
        ],
        compiler_params=pltpu.CompilerParams(
            collective_id=0, has_side_effects=True, vmem_limit_bytes=60_000_000
        ),
        name="moe_layer",
    )(q, dq, dlen, idx.T, gate.T, gain[None], k, v, dk, dv, wg, wu, wd)
    return out[:tokens], out[tokens:]


def solution(mesh):
    both = ("groups", "seq")
    in_specs = (
        P(both, None),
        P(both, None),
        P(both, None),
        P(both, None),
        P(both, None, None),
        P(both, None, None),
        P(both),
        P(both, None),
        P(both, None),
        P(),
        P("seq", None, None),
        P("seq", None, None),
        P("seq", None, None),
    )
    return jax.shard_map(
        functools.partial(on_device, mesh.shape["seq"]),
        mesh=mesh,
        in_specs=in_specs,
        out_specs=(P(both, None), P(both, None)),
        check_vma=False,
    )
```
